256 devices in a mesh: inline: 32 (over x, y, core), xline: 8 (over z).
Axes of the slice: x: 4, y: 4, z: 8, core: 2. Of those that a mesh axis runs over, the one named last changes fastest.
Arguments:
- traces: bfloat16 [65536, 2048], P(('inline', 'xline')), may hold values from -6 to 6
- owners: int32 [65536, 1], P(('inline', 'xline')), may hold values from 0 to 255, as said below
- midpoint: int32 [65536], P(('inline', 'xline')), may hold values from 0 to 7
- offset_class: int32 [65536], P(('inline', 'xline')), may hold values from 0 to 3
- offsets: float32 [4], replicated, may hold values from 51 to 1024
- velocities: float32 [16], replicated, may hold values from 1 to 4
Outputs:
- stacked: bfloat16 [2048, 16, 2048], P(('inline', 'xline'))
- semblance: float32 [2048, 16, 2048], P(('inline', 'xline'))
The draws below stay inside these ranges and needn't reach their ends.
Inputs may be any that keep to these rules, and one draw needn't show every extreme that they name: The 256 traces of one device name one owner at most 2 times; some owners receive 2 traces from every device, and some owners receive none.
All inputs are finite; a program needn't handle non-finite values.
Results may differ from the reference program's by a relative error of at most 0.0053.
Values may be sent and summed in bfloat16 or wider, within the bound.
A program may use at most 64 MiB of HBM per device.

```python
import math
import jax
import jax.numpy as jnp
from jax import lax

NT = 2048
VEL = 16
H = 4
HALF_WIN = 4
TR_DEV = 256
CMP_DEV = 8
CAP = 2
TRACES = 65536
NCMP = 2048
DEVICES = 256


def draw_owners(key, part):
    slot_count = DEVICES * CAP
    base_key = jax.random.fold_in(key, 7301)
    key_pair, key_single, key_order, key_level, key_rows = jax.random.split(base_key, 5)
    first_dead = jax.random.randint(key_pair, (), 0, DEVICES - 1)
    lone_dead = (first_dead + 2 + jax.random.randint(key_single, (), 0, DEVICES - 2)) % DEVICES
    owner_ids = jnp.arange(DEVICES)
    dead_owner = (owner_ids == first_dead) | (owner_ids == first_dead + 1) | (owner_ids == lone_dead)
    priority = jax.random.permutation(key_order, DEVICES)
    busiest_owner = (priority < max(1, DEVICES // 16) + 3) & jnp.logical_not(dead_owner)
    workload_level = jax.random.randint(key_level, (DEVICES,), 0, 4)
    reward_score = jnp.where(busiest_owner, 16384, workload_level * 256)
    position_owner = jnp.arange(slot_count) // CAP
    position_empty = dead_owner[position_owner]
    position_reward = reward_score[position_owner]

    def one_block(block_key):
        key_score, key_shuffle = jax.random.split(block_key)
        random_perturbation = jax.random.randint(key_score, (slot_count,), 0, 1024)
        position_score = jnp.where(position_empty, -1, position_reward + random_perturbation)
        distinct = position_score * slot_count + jnp.arange(slot_count)
        chosen = lax.top_k(distinct, TR_DEV)[1]
        return jax.random.permutation(key_shuffle, chosen // CAP)
    blocks = jax.vmap(one_block)(jax.random.split(key_rows, DEVICES))
    return blocks.reshape(TRACES, 1).astype(jnp.int32)


def with_ends(drawn, key, smallest, high):
    longest = drawn.shape.index(max(drawn.shape))
    spots = []
    for shift in (0, 1):
        where = [jax.random.randint(jax.random.fold_in(key, axis), (), 0, length) for axis, length in enumerate(drawn.shape)]
        where[longest] = (where[longest] + shift) % drawn.shape[longest]
        spots.append(tuple(where))
    return drawn.at[spots[0]].set(smallest).at[spots[1]].set(high)


def levels(key, shape, shards, low, largest):
    level = 1.0
    for axis_at, shards_of in shards:
        heights = jax.random.uniform(jax.random.fold_in(jax.random.fold_in(key, 6), axis_at), (shards_of,), jnp.float32, low / len(shards), largest / len(shards))
        level = level * jnp.repeat(jnp.exp(heights), shape[axis_at] // shards_of).reshape((-1,) + (1,) * (len(shape) - 1 - axis_at))
    return level


def gaussian(rng, shape, deviation, bound, cuts=(), kind=jnp.bfloat16):
    loudness = levels(rng, shape, cuts, -0.22, 0.18) if cuts else 1.0
    result = jax.random.normal(rng, shape, jnp.float32) * deviation * loudness
    return jnp.minimum(jnp.maximum(result, -bound), bound).astype(kind)


def setup_inputs(seed: int = 0) -> dict:
    keys = jax.random.split(jax.random.key(seed), 7)
    return {
        "traces": gaussian(keys[0], (TRACES, NT), 1.0, 6.0, ((0, 256),)),
        "owners": draw_owners(jax.random.fold_in(keys[6], 71), 0),
        "midpoint": with_ends(jax.random.randint(keys[2], (TRACES,), 0, CMP_DEV), jax.random.fold_in(keys[2], 1), 0, CMP_DEV - 1).astype(jnp.int32),
        "offset_class": with_ends(jax.random.randint(keys[3], (TRACES,), 0, H), jax.random.fold_in(keys[3], 1), 0, H - 1).astype(jnp.int32),
        "offsets": jnp.clip(jax.random.uniform(keys[4], (H,), jnp.float32, 51.0, 1024.0), 51.0, 1024.0),
        "velocities": jnp.clip(jnp.exp(jax.random.uniform(keys[5], (VEL,), jnp.float32, math.log(1.0), math.log(4.0))), 1.0, 4.0),
    }


def window_sum(values):
    length = values.shape[-1]
    padded = jnp.pad(values, [(0, 0)] * (values.ndim - 1) + [(HALF_WIN, HALF_WIN)])
    summed = padded[..., 0:length]
    for offset in range(1, 2 * HALF_WIN + 1):
        summed = summed + padded[..., offset:offset + length]
    return summed

def neighbour_sum(values):
    padded = jnp.pad(values, ((1, 1), (0, 0)))
    return padded[0:-2] + padded[1:-1] + padded[2:]

def reference(traces, owners, midpoint, offset_class, offsets, velocities):
    classes = offsets.shape[0]
    samples = traces.shape[1]
    global_mid = owners[:, 0] * CMP_DEV + midpoint
    slot_keys = global_mid * classes + offset_class
    block_rows = TR_DEV * math.gcd(DEVICES, 16)

    def add_block(running, pieces):
        part_traces, part_keys = pieces
        return (running + jax.ops.segment_sum(part_traces.astype(jnp.float32), part_keys, NCMP * classes), None)
    start_sum = jnp.zeros((NCMP * classes, samples), jnp.float32)
    gathers, _ = lax.scan(add_block, start_sum, (traces.reshape(-1, block_rows, samples), slot_keys.reshape(-1, block_rows)))
    binned = lax.optimization_barrier(gathers.astype(jnp.bfloat16)).astype(jnp.float32).reshape(NCMP, classes, samples)
    fold_count = jax.ops.segment_sum(jnp.ones(midpoint.shape, jnp.float32), global_mid, NCMP)
    padded = jnp.pad(binned, ((0, 0), (0, 0), (0, 2)))
    sample_time = jnp.arange(samples).astype(jnp.float32)
    shaped = (NCMP, classes, samples)

    def per_velocity(velocity):
        slowness = offsets / velocity
        position = jnp.sqrt(sample_time[None, :] * sample_time[None, :] + (slowness * slowness)[:, None])
        floored = jnp.floor(position)
        fraction = position - floored
        sample_index = jnp.minimum(floored, float(samples)).astype(jnp.int32)
        low_weight = lax.optimization_barrier((1.0 - fraction).astype(jnp.bfloat16)).astype(jnp.float32)
        high_weight = lax.optimization_barrier(fraction.astype(jnp.bfloat16)).astype(jnp.float32)
        lower_val = jnp.take_along_axis(padded, jnp.broadcast_to(sample_index[None], shaped), axis=2)
        upper_val = jnp.take_along_axis(padded, jnp.broadcast_to(sample_index[None] + 1, shaped), axis=2)
        moved_out = low_weight[None] * lower_val + high_weight[None] * upper_val
        summed = lax.optimization_barrier(jnp.sum(moved_out, axis=1))
        energy = lax.optimization_barrier(jnp.sum(moved_out * moved_out, axis=1))
        stacked = (summed / jnp.maximum(fold_count, 1.0)[:, None]).astype(jnp.bfloat16)
        numerator = neighbour_sum(window_sum(summed * summed))
        denominator = neighbour_sum(window_sum(energy))
        return (stacked, numerator / jnp.maximum(classes * denominator, 1.0))
    stacked, semblance = lax.map(per_velocity, velocities)
    return (jnp.transpose(stacked, (1, 0, 2)), jnp.transpose(semblance, (1, 0, 2)))
```

```python
import functools

import jax
import jax.numpy as jnp
from jax import lax
from jax.experimental import pallas as pl
from jax.experimental.pallas import tpu as pltpu
from jax.sharding import PartitionSpec as P

CMP_DEV = 8

LANES = 128
GROUP = 8


def take_lanes(values, index):
    return jnp.take_along_axis(values, index, axis=1, mode="promise_in_bounds")


def panels_kernel(
    start_ref, slow_ref, x_ref, fold_ref, stacked_ref, semblance_ref,
    low_at, high_at, low_w, high_w, power, energy, sums, ratio,
):
    vels, mids, samples = semblance_ref.shape[1], semblance_ref.shape[0], semblance_ref.shape[2]
    classes = x_ref.shape[0]
    blocks = samples // LANES

    def prepare(gh, _):
        row = lax.broadcasted_iota(jnp.int32, (blocks, LANES), 0)
        lane = lax.broadcasted_iota(jnp.int32, (blocks, LANES), 1)
        time = (row * LANES + lane).astype(jnp.float32)
        position = jnp.sqrt(time * time + slow_ref[gh])
        floored = jnp.floor(position)
        fraction = position - floored
        index = jnp.minimum(floored, float(samples)).astype(jnp.int32)
        rows = pl.ds(pl.multiple_of(gh * blocks, blocks), blocks)
        low_at[rows, :] = index & (LANES - 1)
        high_at[rows, :] = (index + 1) & (LANES - 1)
        low_w[rows, :] = (1.0 - fraction).astype(jnp.bfloat16).astype(jnp.float32)
        high_w[rows, :] = fraction.astype(jnp.bfloat16).astype(jnp.float32)
        return 0

    lax.fori_loop(0, vels * classes, prepare, 0)

    edge = jnp.zeros((mids, LANES), jnp.float32)
    for g in range(vels):
        for plane in (power, energy):
            plane[g * mids:(g + 1) * mids, 0:LANES] = edge
            plane[g * mids:(g + 1) * mids, LANES + samples:] = edge

    shape = (mids, LANES)
    lane = lax.broadcasted_iota(jnp.int32, shape, 1)
    sub = lax.broadcasted_iota(jnp.int32, shape, 0)
    scale = 1.0 / jnp.maximum(fold_ref[...], 1.0)

    def three(own, rim):
        up = pltpu.roll(jnp.where(sub == mids - 1, rim, own), 1, 0)
        down = pltpu.roll(jnp.where(sub == 0, rim, own), mids - 1, 0)
        return own + up + down

    def stack(gb, _):
        g, b = gb // blocks, gb % blocks
        total = jnp.zeros(shape, jnp.float32)
        square = jnp.zeros(shape, jnp.float32)
        rim_total = jnp.zeros(shape, jnp.float32)
        rim_square = jnp.zeros(shape, jnp.float32)
        for h in range(classes):
            row = (g * classes + h) * blocks + b
            start = start_ref[row]
            first = pl.multiple_of((start // LANES) * LANES, LANES)
            second = pl.multiple_of(first + LANES, LANES)
            offset = start % LANES
            low_mask = lane >= offset
            high_mask = lane > offset
            bc = lambda ref: jnp.broadcast_to(ref[pl.ds(row, 1), :], shape)
            li, hi, lw, hw = bc(low_at), bc(high_at), bc(low_w), bc(high_w)
            for at, is_rim in ((0, False), (mids, True)):
                near = x_ref[h, at:at + mids, pl.ds(first, LANES)]
                far = x_ref[h, at:at + mids, pl.ds(second, LANES)]
                moved = lw * take_lanes(jnp.where(low_mask, near, far), li) + hw * take_lanes(
                    jnp.where(high_mask, near, far), hi
                )
                if is_rim:
                    rim_total += moved
                    rim_square += moved * moved
                else:
                    total += moved
                    square += moved * moved
        rows = pl.ds(pl.multiple_of(g * mids, mids), mids)
        shifted = pl.ds(pl.multiple_of(b * LANES + LANES, LANES), LANES)
        sums[b, rows, :] = total * scale
        power[rows, shifted] = three(total * total, rim_total * rim_total)
        energy[rows, shifted] = three(square, rim_square)
        return 0

    lax.fori_loop(0, vels * blocks, stack, 0)

    width = samples + 2 * LANES

    def window(plane):
        by3 = plane + pltpu.roll(plane, 1, 1) + pltpu.roll(plane, width - 1, 1)
        by9 = by3 + pltpu.roll(by3, 3, 1) + pltpu.roll(by3, width - 3, 1)
        return by9[:, LANES:LANES + samples]

    def finish(g, _):
        rows = pl.ds(pl.multiple_of(g * mids, mids), mids)
        top = window(power[rows, :])
        bottom = window(energy[rows, :])
        value = top / jnp.maximum(classes * bottom, 1.0)
        for b in range(blocks):
            ratio[b, rows, :] = value[:, b * LANES:(b + 1) * LANES]
        return 0

    lax.fori_loop(0, vels, finish, 0)

    def turn(b, _):
        columns = pl.ds(pl.multiple_of(b * LANES, LANES), LANES)
        for m in range(mids):
            for half in range(vels // GROUP):
                semblance_ref[m, half * GROUP:(half + 1) * GROUP, columns] = ratio[
                    b, pl.ds(half * GROUP * mids + m, GROUP, stride=mids), :]
            stacked_ref[m, :, columns] = jnp.concatenate([
                sums[b, pl.ds(half * GROUP * mids + m, GROUP, stride=mids), :]
                for half in range(vels // GROUP)
            ], axis=0).astype(jnp.bfloat16)
        return 0

    lax.fori_loop(0, blocks, turn, 0)


def panels(x, fold, offsets, velocities, samples):
    classes, rows, _ = x.shape
    mids = rows // 2
    vels = velocities.shape[0]
    blocks = samples // LANES
    slowness = offsets[None, :] / velocities[:, None]
    slow = slowness * slowness
    time = (jnp.arange(blocks) * LANES).astype(jnp.float32)
    position = jnp.sqrt(time * time + slow[:, :, None])
    start = jnp.minimum(jnp.floor(position), float(samples)).astype(jnp.int32).reshape(-1)
    smem = pl.BlockSpec(memory_space=pltpu.SMEM)
    vmem = pl.BlockSpec(memory_space=pltpu.VMEM)
    count = vels * classes * blocks
    return pl.pallas_call(
        panels_kernel,
        out_shape=(
            jax.ShapeDtypeStruct((mids, vels, samples), jnp.bfloat16),
            jax.ShapeDtypeStruct((mids, vels, samples), jnp.float32),
        ),
        in_specs=[smem, smem, vmem, vmem],
        out_specs=(vmem, vmem),
        scratch_shapes=[
            pltpu.VMEM((count, LANES), jnp.int32),
            pltpu.VMEM((count, LANES), jnp.int32),
            pltpu.VMEM((count, LANES), jnp.float32),
            pltpu.VMEM((count, LANES), jnp.float32),
            pltpu.VMEM((vels * mids, samples + 2 * LANES), jnp.float32),
            pltpu.VMEM((vels * mids, samples + 2 * LANES), jnp.float32),
            pltpu.VMEM((blocks, vels * mids, LANES), jnp.float32),
            pltpu.VMEM((blocks, vels * mids, LANES), jnp.float32),
        ],
        name="panels",
    )(start, slow.reshape(-1), x, fold)


def per_device(traces, owners, midpoint, offset_class, offsets, velocities):
    inline_count = lax.axis_size("inline")
    xline_count = lax.axis_size("xline")
    devices = inline_count * xline_count
    axes = ("inline", "xline")
    me = lax.axis_index(axes)
    trace_rows, samples = traces.shape
    classes = offsets.shape[0]
    capacity = max(2, 2 * trace_rows // devices)
    target = owners[:, 0]
    onehot_dest = (target[:, None] == jnp.arange(devices)[None, :]).astype(jnp.int32)
    slot_rank = jnp.sum((jnp.cumsum(onehot_dest, axis=0) - onehot_dest) * onehot_dest, axis=1)
    slot_row = target * capacity + slot_rank
    buffer = jnp.zeros((devices * capacity, samples), traces.dtype).at[slot_row].set(traces)
    slot_keys = (
        jnp.full((devices * capacity,), -1, jnp.int32)
        .at[slot_row]
        .set(offset_class * CMP_DEV + midpoint)
    )
    buffer = buffer.reshape(inline_count, xline_count, capacity, samples)
    slot_keys = slot_keys.reshape(inline_count, xline_count, capacity)

    def exchange(block):
        block = lax.all_to_all(block, "inline", split_axis=0, concat_axis=0, tiled=True)
        return lax.all_to_all(block, "xline", split_axis=1, concat_axis=1, tiled=True)

    arrived_keys = exchange(slot_keys).reshape(-1)
    arrived = exchange(buffer).reshape(-1, samples)
    members = arrived_keys[None, :] == jnp.arange(classes * CMP_DEV)[:, None]
    gathers = jnp.dot(members.astype(jnp.bfloat16), arrived, preferred_element_type=jnp.float32)
    binned = gathers.astype(jnp.bfloat16).reshape(classes, CMP_DEV, samples)
    counts = jnp.sum(members.astype(jnp.float32), axis=1).reshape(classes, CMP_DEV)
    fold = jnp.broadcast_to(jnp.sum(counts, axis=0)[:, None], (CMP_DEV, LANES))
    forward = [(i, i + 1) for i in range(devices - 1)]
    backward = [(i + 1, i) for i in range(devices - 1)]
    left = lax.ppermute(binned[:, CMP_DEV - 1:], axes, forward)
    right = lax.ppermute(binned[:, :1], axes, backward)
    middle = jnp.zeros((classes, CMP_DEV - 2, samples), binned.dtype)
    x = jnp.concatenate([binned, right, middle, left], axis=1).astype(jnp.float32)
    x = jnp.pad(x, ((0, 0), (0, 0), (0, 2 * LANES)))
    return panels(x, fold, offsets, velocities, samples)


def solution(mesh):
    in_specs = (
        P(("inline", "xline"), None),
        P(("inline", "xline"), None),
        P(("inline", "xline")),
        P(("inline", "xline")),
        P(),
        P(),
    )
    out_specs = (P(("inline", "xline"), None, None), P(("inline", "xline"), None, None))
    return jax.shard_map(
        per_device, mesh=mesh, in_specs=in_specs, out_specs=out_specs, check_vma=False
    )
```

```python
import functools

import jax
import jax.numpy as jnp
from jax import lax
from jax.experimental import pallas as pl
from jax.experimental.pallas import tpu as pltpu
from jax.sharding import PartitionSpec as P

CMP_DEV = 8

LANES = 128
GROUP = 8


def take_lanes(values, index):
    return jnp.take_along_axis(values, index, axis=1, mode="promise_in_bounds")


def panels_kernel(
    start_ref, slow_ref, x_ref, fold_ref, stacked_ref, semblance_ref,
    low_at, high_at, low_w, high_w, power, energy, sums, ratio,
):
    vels, mids, samples = semblance_ref.shape[1], semblance_ref.shape[0], semblance_ref.shape[2]
    classes = x_ref.shape[0]
    blocks = samples // LANES

    def prepare(step, _):
        for part in range(4):
            prepare_one(step * 4 + part)
        return 0

    def prepare_one(gh):
        row = lax.broadcasted_iota(jnp.int32, (blocks, LANES), 0)
        lane = lax.broadcasted_iota(jnp.int32, (blocks, LANES), 1)
        time = (row * LANES + lane).astype(jnp.float32)
        position = jnp.sqrt(time * time + slow_ref[gh])
        floored = jnp.floor(position)
        fraction = position - floored
        index = jnp.minimum(floored, float(samples)).astype(jnp.int32)
        rows = pl.ds(pl.multiple_of(gh * blocks, blocks), blocks)
        low_at[rows, :] = index & (LANES - 1)
        high_at[rows, :] = (index + 1) & (LANES - 1)
        low_w[rows, :] = (1.0 - fraction).astype(jnp.bfloat16).astype(jnp.float32)
        high_w[rows, :] = fraction.astype(jnp.bfloat16).astype(jnp.float32)

    lax.fori_loop(0, vels * classes // 4, prepare, 0)

    edge = jnp.zeros((mids, LANES), jnp.float32)
    for g in range(vels):
        for plane in (power, energy):
            plane[g * mids:(g + 1) * mids, 0:LANES] = edge
            plane[g * mids:(g + 1) * mids, LANES + samples:] = edge

    shape = (mids, LANES)
    lane = lax.broadcasted_iota(jnp.int32, shape, 1)
    sub = lax.broadcasted_iota(jnp.int32, shape, 0)
    scale = 1.0 / jnp.maximum(fold_ref[...], 1.0)

    def three(own, rim):
        up = pltpu.roll(jnp.where(sub == mids - 1, rim, own), 1, 0)
        down = pltpu.roll(jnp.where(sub == 0, rim, own), mids - 1, 0)
        return own + up + down

    def stack(step, _):
        g = step >> 2
        for part in range(blocks // 4):
            stack_one(g, (step & 3) * (blocks // 4) + part)
        return 0

    def stack_one(g, b):
        total = jnp.zeros(shape, jnp.float32)
        square = jnp.zeros(shape, jnp.float32)
        rim_total = jnp.zeros(shape, jnp.float32)
        rim_square = jnp.zeros(shape, jnp.float32)
        for h in range(classes):
            row = (g * classes + h) * blocks + b
            start = start_ref[row]
            first = pl.multiple_of((start >> 7) << 7, LANES)
            second = pl.multiple_of(first + LANES, LANES)
            offset = start & (LANES - 1)
            low_mask = lane >= offset
            high_mask = lane > offset
            bc = lambda ref: jnp.broadcast_to(ref[pl.ds(row, 1), :], shape)
            li, hi, lw, hw = bc(low_at), bc(high_at), bc(low_w), bc(high_w)
            for at, is_rim in ((0, False), (mids, True)):
                near = x_ref[h, at:at + mids, pl.ds(first, LANES)]
                far = x_ref[h, at:at + mids, pl.ds(second, LANES)]
                moved = lw * take_lanes(jnp.where(low_mask, near, far), li) + hw * take_lanes(
                    jnp.where(high_mask, near, far), hi
                )
                if is_rim:
                    rim_total += moved
                    rim_square += moved * moved
                else:
                    total += moved
                    square += moved * moved
        rows = pl.ds(pl.multiple_of(g * mids, mids), mids)
        shifted = pl.ds(pl.multiple_of(b * LANES + LANES, LANES), LANES)
        sums[b, rows, :] = total * scale
        power[rows, shifted] = three(total * total, rim_total * rim_total)
        energy[rows, shifted] = three(square, rim_square)

    lax.fori_loop(0, vels * 4, stack, 0)

    width = samples + 2 * LANES

    def window(plane):
        by3 = plane + pltpu.roll(plane, 1, 1) + pltpu.roll(plane, width - 1, 1)
        by9 = by3 + pltpu.roll(by3, 3, 1) + pltpu.roll(by3, width - 3, 1)
        return by9[:, LANES:LANES + samples]

    def finish(g, _):
        rows = pl.ds(pl.multiple_of(g * mids, mids), mids)
        top = window(power[rows, :])
        bottom = window(energy[rows, :])
        value = top / jnp.maximum(classes * bottom, 1.0)
        for b in range(blocks):
            ratio[b, rows, :] = value[:, b * LANES:(b + 1) * LANES]
        return 0

    lax.fori_loop(0, vels, finish, 0)

    def turn(b, _):
        columns = pl.ds(pl.multiple_of(b * LANES, LANES), LANES)
        for m in range(mids):
            for half in range(vels // GROUP):
                semblance_ref[m, half * GROUP:(half + 1) * GROUP, columns] = ratio[
                    b, pl.ds(half * GROUP * mids + m, GROUP, stride=mids), :]
            stacked_ref[m, :, columns] = jnp.concatenate([
                sums[b, pl.ds(half * GROUP * mids + m, GROUP, stride=mids), :]
                for half in range(vels // GROUP)
            ], axis=0).astype(jnp.bfloat16)
        return 0

    lax.fori_loop(0, blocks, turn, 0)


def panels(x, fold, offsets, velocities, samples):
    classes, rows, _ = x.shape
    mids = rows // 2
    vels = velocities.shape[0]
    blocks = samples // LANES
    slowness = offsets[None, :] / velocities[:, None]
    slow = slowness * slowness
    time = (jnp.arange(blocks) * LANES).astype(jnp.float32)
    position = jnp.sqrt(time * time + slow[:, :, None])
    start = jnp.minimum(jnp.floor(position), float(samples)).astype(jnp.int32).reshape(-1)
    smem = pl.BlockSpec(memory_space=pltpu.SMEM)
    vmem = pl.BlockSpec(memory_space=pltpu.VMEM)
    count = vels * classes * blocks
    return pl.pallas_call(
        panels_kernel,
        out_shape=(
            jax.ShapeDtypeStruct((mids, vels, samples), jnp.bfloat16),
            jax.ShapeDtypeStruct((mids, vels, samples), jnp.float32),
        ),
        in_specs=[smem, smem, vmem, vmem],
        out_specs=(vmem, vmem),
        scratch_shapes=[
            pltpu.VMEM((count, LANES), jnp.int32),
            pltpu.VMEM((count, LANES), jnp.int32),
            pltpu.VMEM((count, LANES), jnp.float32),
            pltpu.VMEM((count, LANES), jnp.float32),
            pltpu.VMEM((vels * mids, samples + 2 * LANES), jnp.float32),
            pltpu.VMEM((vels * mids, samples + 2 * LANES), jnp.float32),
            pltpu.VMEM((blocks, vels * mids, LANES), jnp.float32),
            pltpu.VMEM((blocks, vels * mids, LANES), jnp.float32),
        ],
        name="panels",
    )(start, slow.reshape(-1), x, fold)

MESH = pl.DeviceIdType.MESH
CHUNKS = 4
TILE = 256


def gather_kernel(
    dims, traces_ref, owner_ref, key_ref, x_ref, fold_ref,
    buf, arr, kout, karr, member, zout, zarr, cout, carr, eout, earr,
    plane_send, plane_recv, zed_send, zed_recv, rim_send, rim_recv, own_sem,
):
    nx, ny, nz = dims
    inline = nx * ny * 2
    rows, samples = traces_ref.shape
    slots = buf.shape[0] // inline
    bins = zout.shape[1]
    classes = x_ref.shape[0]
    mids = bins // classes
    width = samples // CHUNKS
    tile = min(TILE, width)
    me, mz = lax.axis_index("inline"), lax.axis_index("xline")
    mx, my, mc = me // (2 * ny), (me // 2) % ny, me % 2

    def plane_peer(p, sign):
        q = p // 2
        dx = q % nx
        dy = (q // nx + dx) % ny
        px = (mx + nx + sign * dx) % nx
        py = (my + ny + sign * dy) % ny
        return (px * ny + py) * 2 + (mc + p) % 2

    def zed_peer(p):
        step = (p + 1) // 2
        return (mz + jnp.where(p % 2 == 1, step, nz - step)) % nz

    right = (lax.rem(me + jnp.where(mz == nz - 1, 1, 0), inline), lax.rem(mz + 1, nz))
    left = (lax.rem(me + jnp.where(mz == 0, inline - 1, 0), inline), lax.rem(mz + nz - 1, nz))

    barrier = pltpu.get_barrier_semaphore()

    def greet_plane(p, _):
        pl.semaphore_signal(barrier, inc=1, device_id=(plane_peer(p, 1), mz), device_id_type=MESH)
        return 0

    def greet_zed(p, _):
        pl.semaphore_signal(barrier, inc=1, device_id=(me, zed_peer(p)), device_id_type=MESH)
        return 0

    lax.fori_loop(1, inline, greet_plane, 0)
    lax.fori_loop(1, nz, greet_zed, 0)
    for peer in (left, right):
        pl.semaphore_signal(barrier, inc=1, device_id=peer, device_id_type=MESH)

    square = (rows, rows)
    first = lax.broadcasted_iota(jnp.int32, square, 0)
    second = lax.broadcasted_iota(jnp.int32, square, 1)
    owner_row = owner_ref[...]
    owner_all = jnp.broadcast_to(owner_row.astype(jnp.float32), square)
    owner_col = jnp.sum(jnp.where(first == second, owner_all, 0.0), axis=1, keepdims=True)
    same = owner_all == owner_col
    rank_row = jnp.sum(jnp.where(same & (first < second), 1.0, 0.0), axis=0, keepdims=True).astype(jnp.int32)
    rank_col = jnp.sum(jnp.where(same & (second < first), 1.0, 0.0), axis=1, keepdims=True).astype(jnp.int32)
    capacity = slots // nz
    slot_row = owner_row * capacity + rank_row
    wide = (buf.shape[0], rows)
    member_out = jnp.where(
        lax.broadcasted_iota(jnp.int32, wide, 0) == slot_row, 1.0, 0.0).astype(jnp.bfloat16)
    per_lane = 128 // slots
    owner_col = owner_col.astype(jnp.int32)
    lane_at = (me % per_lane) * slots + (owner_col % nz) * capacity + rank_col
    placed = jnp.where(
        lax.broadcasted_iota(jnp.int32, (rows, 128), 1) == lane_at, 1.0, 0.0).astype(jnp.bfloat16)
    number = ((owner_row % nz) * bins + key_ref[...] + 1).astype(jnp.float32)
    chosen = jnp.where(
        lax.broadcasted_iota(jnp.int32, (inline, rows), 0) == owner_row // nz, number, 0.0
    ).astype(jnp.bfloat16)
    keys = jnp.dot(chosen, placed, preferred_element_type=jnp.float32)
    for i in range(inline):
        kout[i] = keys[i:i + 1, :]
    member[0:buf.shape[0], 0:rows] = member_out

    def place(t, _):
        columns = pl.ds(pl.multiple_of(t * tile, tile), tile)
        buf[:, columns] = jnp.dot(
            member[0:buf.shape[0], 0:rows], traces_ref[:, columns],
            preferred_element_type=jnp.float32).astype(jnp.bfloat16)
        return 0

    lax.fori_loop(0, samples // tile, place, 0)

    pl.semaphore_wait(barrier, inline - 1 + nz - 1 + 2)

    own = pl.ds(pl.multiple_of(me * slots, slots), slots)
    own_copy = pltpu.make_async_copy(buf.at[own, :], arr.at[own, :], own_sem)
    own_copy.start()

    def send_key(p, _):
        peer = plane_peer(p, 1)
        pltpu.make_async_remote_copy(
            src_ref=kout.at[peer], dst_ref=karr.at[me],
            send_sem=plane_send.at[CHUNKS], recv_sem=plane_recv.at[CHUNKS],
            device_id=(peer, mz), device_id_type=MESH).start()
        return 0

    lax.fori_loop(1, inline, send_key, 0)

    def cut(c):
        return pl.ds(c * width, width)

    for c in range(CHUNKS):
        def send_plane(p, _, c=c):
            peer = plane_peer(p, 1)
            pltpu.make_async_remote_copy(
                src_ref=buf.at[pl.ds(pl.multiple_of(peer * slots, slots), slots), cut(c)],
                dst_ref=arr.at[own, cut(c)],
                send_sem=plane_send.at[c], recv_sem=plane_recv.at[c],
                device_id=(peer, mz), device_id_type=MESH).start()
            return 0
        lax.fori_loop(1, inline, send_plane, 0)

    def all_of(ref, sem):
        pltpu.make_async_copy(ref, ref, sem).wait()

    karr[me] = kout[me]
    all_of(karr.at[pl.ds(0, inline - 1)], plane_recv.at[CHUNKS])
    for q in range(inline // per_lane):
        line = karr[q * per_lane]
        for s in range(1, per_lane):
            line = line + karr[q * per_lane + s]
        number_at = lax.broadcasted_iota(jnp.int32, (nz * bins, 128), 0) + 1
        member[0:nz * bins, q * 128:(q + 1) * 128] = jnp.where(
            line.astype(jnp.int32) == number_at, 1.0, 0.0).astype(jnp.bfloat16)
    arrived_rows = inline * slots
    counts = jnp.dot(
        member[0:nz * bins, 0:arrived_rows], jnp.ones((arrived_rows, 128), jnp.bfloat16),
        preferred_element_type=jnp.float32)
    for z in range(nz):
        cout[z] = counts[z * bins:(z + 1) * bins]
    carr[mz] = cout[mz]

    def send_count(p, _):
        peer = zed_peer(p)
        pltpu.make_async_remote_copy(
            src_ref=cout.at[peer], dst_ref=carr.at[mz],
            send_sem=zed_send.at[CHUNKS], recv_sem=zed_recv.at[CHUNKS],
            device_id=(me, peer), device_id_type=MESH).start()
        return 0

    own_copy.wait()

    def bin_chunk(c):
        all_of(arr.at[pl.ds(0, (inline - 1) * slots), cut(c)], plane_recv.at[c])

        def bin_tile(t, _):
            columns = pl.ds(pl.multiple_of(c * width + t * tile, tile), tile)
            part = jnp.dot(
                member[0:nz * bins, 0:arrived_rows], arr[:, columns],
                preferred_element_type=jnp.float32).astype(jnp.bfloat16)
            for z in range(nz):
                zout[z, :, columns] = part[z * bins:(z + 1) * bins]
            return 0

        lax.fori_loop(0, width // tile, bin_tile, 0)
        zarr[mz, :, cut(c)] = zout[mz, :, cut(c)]
        if c == 0:
            lax.fori_loop(1, nz, send_count, 0)

        def send_zed(p, _):
            peer = zed_peer(p)
            pltpu.make_async_remote_copy(
                src_ref=zout.at[peer, :, cut(c)], dst_ref=zarr.at[mz, :, cut(c)],
                send_sem=zed_send.at[c], recv_sem=zed_recv.at[c],
                device_id=(me, peer), device_id_type=MESH).start()
            return 0

        lax.fori_loop(1, nz, send_zed, 0)

    def rim_copies(c):
        return [pltpu.make_async_remote_copy(
            src_ref=eout.at[side, :, cut(c)], dst_ref=earr.at[side, :, cut(c)],
            send_sem=rim_send.at[side, c], recv_sem=rim_recv.at[side, c],
            device_id=peer, device_id_type=MESH) for side, peer in ((0, left), (1, right))]

    def sum_chunk(c):
        all_of(zarr.at[pl.ds(0, nz - 1), :, cut(c)], zed_recv.at[c])

        def sum_tile(t, _):
            columns = pl.ds(pl.multiple_of(c * width + t * 128, 128), 128)
            total = zarr[0, :, columns].astype(jnp.float32)
            for z in range(1, nz):
                total = total + zarr[z, :, columns].astype(jnp.float32)
            total = total.astype(jnp.bfloat16).astype(jnp.float32)
            for h in range(classes):
                part = total[h * mids:(h + 1) * mids]
                x_ref[h, 0:mids, columns] = part
                eout[0, h:h + 1, columns] = part[0:1]
                eout[1, h:h + 1, columns] = part[mids - 1:mids]
            return 0

        lax.fori_loop(0, width // 128, sum_tile, 0)
        for copy in rim_copies(c):
            copy.start()

    for c in range(CHUNKS + 1):
        if c < CHUNKS:
            bin_chunk(c)
        if c >= 1:
            sum_chunk(c - 1)

    all_of(carr.at[pl.ds(0, nz - 1)], zed_recv.at[CHUNKS])
    total = carr[0]
    for z in range(1, nz):
        total = total + carr[z]
    fold = total[0:mids]
    for h in range(1, classes):
        fold = fold + total[h * mids:(h + 1) * mids]
    fold_ref[...] = fold

    for h in range(classes):
        x_ref[h, :, samples:] = jnp.zeros((2 * mids, x_ref.shape[2] - samples), jnp.float32)
        x_ref[h, mids:, 0:samples] = jnp.zeros((mids, samples), jnp.float32)
    for c in range(CHUNKS):
        for copy in rim_copies(c):
            copy.wait()
    is_first = (me == 0) & (mz == 0)
    is_last = (me == inline - 1) & (mz == nz - 1)
    for h in range(classes):
        from_right, from_left = earr[0, h:h + 1, :], earr[1, h:h + 1, :]
        x_ref[h, mids:mids + 1, 0:samples] = jnp.where(is_last, jnp.zeros_like(from_right), from_right)
        x_ref[h, 2 * mids - 1:2 * mids, 0:samples] = jnp.where(is_first, jnp.zeros_like(from_left), from_left)

    for c in range(CHUNKS):
        all_of(buf.at[pl.ds(0, (inline - 1) * slots), cut(c)], plane_send.at[c])
        all_of(zout.at[pl.ds(0, nz - 1), :, cut(c)], zed_send.at[c])
    all_of(kout.at[pl.ds(0, inline - 1)], plane_send.at[CHUNKS])
    all_of(cout.at[pl.ds(0, nz - 1)], zed_send.at[CHUNKS])


def gather(dims, traces, owners, keys, classes, mids):
    nx, ny, nz = dims
    inline = nx * ny * 2
    rows, samples = traces.shape
    capacity = max(2, 2 * rows // (inline * nz))
    slots = nz * capacity
    bins = classes * mids
    f32, bf16 = jnp.float32, jnp.bfloat16
    vmem = pl.BlockSpec(memory_space=pltpu.VMEM)
    dma = pltpu.SemaphoreType.DMA
    return pl.pallas_call(
        functools.partial(gather_kernel, dims),
        out_shape=(
            jax.ShapeDtypeStruct((classes, 2 * mids, samples + 2 * LANES), f32),
            jax.ShapeDtypeStruct((mids, LANES), f32),
        ),
        in_specs=[vmem] * 3,
        out_specs=(vmem, vmem),
        scratch_shapes=[
            pltpu.VMEM((inline * slots, samples), bf16),
            pltpu.VMEM((inline * slots, samples), bf16),
            pltpu.VMEM((inline, 1, 128), f32),
            pltpu.VMEM((inline, 1, 128), f32),
            pltpu.VMEM((max(inline * slots, nz * bins), max(rows, inline * slots)), bf16),
            pltpu.VMEM((nz, bins, samples), bf16),
            pltpu.VMEM((nz, bins, samples), bf16),
            pltpu.VMEM((nz, bins, 128), f32),
            pltpu.VMEM((nz, bins, 128), f32),
            pltpu.VMEM((2, classes, samples), f32),
            pltpu.VMEM((2, classes, samples), f32),
            dma((CHUNKS + 1,)), dma((CHUNKS + 1,)),
            dma((CHUNKS + 1,)), dma((CHUNKS + 1,)),
            dma((2, CHUNKS)), dma((2, CHUNKS)), dma,
        ],
        compiler_params=pltpu.CompilerParams(collective_id=0, has_side_effects=True),
        name="gather",
    )(traces, owners, keys)


def per_device(traces, owners, midpoint, offset_class, offsets, velocities):
    inline_count = lax.axis_size("inline")
    xline_count = lax.axis_size("xline")
    side = round((inline_count // 2) ** 0.5)
    classes = offsets.shape[0]
    rows, samples = traces.shape
    keys = (offset_class * CMP_DEV + midpoint).reshape(1, rows)
    x, fold = gather(
        (side, side, xline_count), traces, owners.reshape(1, rows), keys, classes, CMP_DEV
    )
    return panels(x, fold, offsets, velocities, samples)


def solution(mesh):
    in_specs = (
        P(("inline", "xline"), None),
        P(("inline", "xline"), None),
        P(("inline", "xline")),
        P(("inline", "xline")),
        P(),
        P(),
    )
    out_specs = (P(("inline", "xline"), None, None), P(("inline", "xline"), None, None))
    return jax.shard_map(
        per_device, mesh=mesh, in_specs=in_specs, out_specs=out_specs, check_vma=False
    )
```

```python
import functools

import jax
import jax.numpy as jnp
from jax import lax
from jax.experimental import pallas as pl
from jax.experimental.pallas import tpu as pltpu
from jax.sharding import PartitionSpec as P

CMP_DEV = 8
LANES = 128
GROUP = 8
MESH = pl.DeviceIdType.MESH


def take_lanes(values, index):
    return lax.gather(
        values, index[:, :, None],
        lax.GatherDimensionNumbers(
            offset_dims=(), collapsed_slice_dims=(1,), start_index_map=(1,),
            operand_batching_dims=(0,), start_indices_batching_dims=(0,)),
        slice_sizes=(1, 1), mode=lax.GatherScatterMode.PROMISE_IN_BOUNDS)


def log2(n):
    assert n & (n - 1) == 0
    return n.bit_length() - 1


def chunks_of(blocks):
    sizes = [2] * ((blocks - 2) // 2) + [1, 1]
    out, top = [], blocks
    for size in sizes:
        top -= size
        out.append((top, size))
    return out


def kernel(
    dims, traces_hbm, owner_ref, midpoint_ref, class_ref, offsets_ref, velocities_ref, start_s, start_v,
    stacked_ref, semblance_ref,
    traces, buf, arr, kout, karr, member, zout, zarr, cout, carr, eout, earr,
    xa, xb, at, low, high, power, energy, sums, ratio,
    plane_send, plane_recv, zed_send, zed_recv, rim_send, rim_recv, own_sem,
):
    nx, ny, nz = dims
    inline = nx * ny * 2
    rows, samples = traces.shape
    slots = buf.shape[0] // inline
    bins = zout.shape[1]
    mids, vels = semblance_ref.shape[:2]
    classes = bins // mids
    blocks = samples // LANES
    plan = chunks_of(blocks)
    last = len(plan)
    me, mz = lax.axis_index("inline"), lax.axis_index("xline")
    mx, my, mc = me >> (log2(ny) + 1), (me >> 1) & (ny - 1), me & 1

    def plane_peer(p):
        q = p >> 1
        tx, ty = q & (nx - 1), q >> log2(nx)
        dx = (nx // 2) ^ tx ^ (tx >> 1)
        dy = (ny // 2) ^ ty ^ (ty >> 1)
        px, py = (mx + dx) & (nx - 1), (my + dy) & (ny - 1)
        return (((px << log2(ny)) | py) << 1) | ((mc + 1 + p) & 1)

    def zed_peer(p):
        step = (p + 1) >> 1
        return (mz + jnp.where((p & 1) == 1, step, nz - step)) & (nz - 1)

    right = ((me + jnp.where(mz == nz - 1, 1, 0)) & (inline - 1), (mz + 1) & (nz - 1))
    left = ((me + jnp.where(mz == 0, inline - 1, 0)) & (inline - 1), (mz + nz - 1) & (nz - 1))

    barrier = pltpu.get_barrier_semaphore()

    def greet_plane(p, _):
        pl.semaphore_signal(barrier, inc=1, device_id=(plane_peer(p), mz), device_id_type=MESH)
        return 0

    def greet_zed(p, _):
        pl.semaphore_signal(barrier, inc=1, device_id=(me, zed_peer(p)), device_id_type=MESH)
        return 0

    traces_in = pltpu.make_async_copy(traces_hbm, traces, own_sem.at[0])
    traces_in.start()
    lax.fori_loop(1, nz, greet_zed, 0)
    lax.fori_loop(0, inline - 1, greet_plane, 0)
    for peer in (left, right):
        pl.semaphore_signal(barrier, inc=1, device_id=peer, device_id_type=MESH)

    square = (rows, rows)
    first = lax.broadcasted_iota(jnp.int32, square, 0)
    second = lax.broadcasted_iota(jnp.int32, square, 1)
    owner_row = owner_ref[...]
    owner_all = jnp.broadcast_to(owner_row.astype(jnp.float32), square)
    owner_col = jnp.sum(jnp.where(first == second, owner_all, 0.0), axis=1, keepdims=True)
    same = owner_all == owner_col
    rank_row = jnp.sum(jnp.where(same & (first < second), 1.0, 0.0), axis=0, keepdims=True).astype(jnp.int32)
    rank_col = jnp.sum(jnp.where(same & (second < first), 1.0, 0.0), axis=1, keepdims=True).astype(jnp.int32)
    capacity = slots // nz
    slot_row = owner_row * capacity + rank_row
    wide = (inline * slots, rows)
    member[0:inline * slots, 0:rows] = jnp.where(
        lax.broadcasted_iota(jnp.int32, wide, 0) == slot_row, 1.0, 0.0).astype(jnp.bfloat16)
    per_lane = 128 // slots
    owner_col = owner_col.astype(jnp.int32)
    lane_at = (me & (per_lane - 1)) * slots + (owner_col & (nz - 1)) * capacity + rank_col
    placed = jnp.where(
        lax.broadcasted_iota(jnp.int32, (rows, 128), 1) == lane_at, 1.0, 0.0).astype(jnp.bfloat16)
    key = class_ref[...] * mids + midpoint_ref[...]
    number = ((owner_row & (nz - 1)) * bins + key + 1).astype(jnp.float32)
    chosen = jnp.where(
        lax.broadcasted_iota(jnp.int32, (inline, rows), 0) == owner_row >> log2(nz), number, 0.0
    ).astype(jnp.bfloat16)
    keys = jnp.dot(chosen, placed, preferred_element_type=jnp.float32)
    for i in range(inline):
        kout[i] = keys[i:i + 1, :]

    def cut(c):
        return pl.ds(plan[c][0] * LANES, plan[c][1] * LANES)

    def place(c):
        buf[:, cut(c)] = jnp.dot(
            member[0:inline * slots, 0:rows], traces[:, cut(c)],
            preferred_element_type=jnp.float32).astype(jnp.bfloat16)

    traces_in.wait()
    place(0)
    place(1)

    def prepare(g, _):
        row = lax.broadcasted_iota(jnp.int32, (blocks, LANES), 0)
        lane = lax.broadcasted_iota(jnp.int32, (blocks, LANES), 1)
        time = (row * LANES + lane).astype(jnp.float32)
        diagonal = lax.broadcasted_iota(jnp.int32, (blocks, blocks), 0) == lax.broadcasted_iota(
            jnp.int32, (blocks, blocks), 1)
        speed = jnp.full((1, LANES), velocities_ref[g])
        for h in range(classes):
            slowness = jnp.full((1, LANES), offsets_ref[h]) / speed
            slow = slowness * slowness
            position = jnp.sqrt(time * time + slow)
            starts = jnp.broadcast_to(
                start_v[pl.ds(g * classes + h, 1), :].astype(jnp.float32), (blocks, blocks))
            starts = jnp.sum(jnp.where(diagonal, starts, 0.0), axis=1, keepdims=True)
            floored = jnp.minimum(jnp.floor(position), float(samples))
            floored = jnp.minimum(jnp.maximum(floored, starts), starts + (LANES - 1))
            fraction = position - floored
            index = floored.astype(jnp.int32)
            here = pl.ds(pl.multiple_of((g * classes + h) * blocks, blocks), blocks)
            at[here, :] = index & (LANES - 1)
            low[here, :] = (1.0 - fraction).astype(jnp.bfloat16).astype(jnp.float32)
            high[here, :] = fraction.astype(jnp.bfloat16).astype(jnp.float32)
        return 0

    lax.fori_loop(0, vels, prepare, 0)

    pl.semaphore_wait(barrier, inline - 1 + nz - 1 + 2)

    own = pl.ds(pl.multiple_of(me * slots, slots), slots)

    def send_plane(c):
        def send(p, _):
            peer = plane_peer(p)
            pltpu.make_async_remote_copy(
                src_ref=buf.at[pl.ds(pl.multiple_of(peer * slots, slots), slots), cut(c)],
                dst_ref=arr.at[own, cut(c)],
                send_sem=plane_send.at[c], recv_sem=plane_recv.at[c],
                device_id=(peer, mz), device_id_type=MESH).start()
            return 0
        lax.fori_loop(0, inline - 1, send, 0)

    def send_key(p, _):
        peer = plane_peer(p)
        pltpu.make_async_remote_copy(
            src_ref=kout.at[peer], dst_ref=karr.at[me],
            send_sem=plane_send.at[last], recv_sem=plane_recv.at[last],
            device_id=(peer, mz), device_id_type=MESH).start()
        return 0

    send_plane(0)
    lax.fori_loop(0, inline - 1, send_key, 0)
    send_plane(1)
    for c in range(2, last):
        place(c)
        send_plane(c)
    own_copy = pltpu.make_async_copy(buf.at[own, :], arr.at[own, :], own_sem.at[1])
    own_copy.start()

    for plane in (power, energy):
        plane[:, 0:LANES] = jnp.zeros((vels * mids, LANES), jnp.float32)
        plane[:, LANES + samples:] = jnp.zeros((vels * mids, LANES), jnp.float32)
    for x in (xa, xb):
        for h in range(classes):
            x[h, :, samples:] = jnp.zeros((2 * mids, 2 * LANES), jnp.float32)

    def all_of(ref, sem):
        pltpu.make_async_copy(ref, ref, sem).wait()

    karr[me] = kout[me]
    all_of(karr.at[pl.ds(0, inline - 1)], plane_recv.at[last])
    arrived = inline * slots
    for q in range(inline // per_lane):
        line = karr[q * per_lane]
        for s in range(1, per_lane):
            line = line + karr[q * per_lane + s]
        number_at = lax.broadcasted_iota(jnp.int32, (nz * bins, 128), 0) + 1
        member[0:nz * bins, q * 128:(q + 1) * 128] = jnp.where(
            line.astype(jnp.int32) == number_at, 1.0, 0.0).astype(jnp.bfloat16)
    counts = jnp.dot(
        member[0:nz * bins, 0:arrived], jnp.ones((arrived, 128), jnp.bfloat16),
        preferred_element_type=jnp.float32)
    for z in range(nz):
        cout[z] = counts[z * bins:(z + 1) * bins]
    carr[mz] = cout[mz]
    own_copy.wait()

    def send_count(p, _):
        peer = zed_peer(p)
        pltpu.make_async_remote_copy(
            src_ref=cout.at[peer], dst_ref=carr.at[mz],
            send_sem=zed_send.at[last], recv_sem=zed_recv.at[last],
            device_id=(me, peer), device_id_type=MESH).start()
        return 0

    def bin_chunk(c):
        all_of(arr.at[pl.ds(0, (inline - 1) * slots), cut(c)], plane_recv.at[c])
        part = jnp.dot(
            member[0:nz * bins, 0:arrived], arr[:, cut(c)],
            preferred_element_type=jnp.float32).astype(jnp.bfloat16)
        for z in range(nz):
            zout[z, :, cut(c)] = part[z * bins:(z + 1) * bins]

        def send(p, _):
            peer = zed_peer(p)
            pltpu.make_async_remote_copy(
                src_ref=zout.at[peer, :, cut(c)], dst_ref=zarr.at[mz, :, cut(c)],
                send_sem=zed_send.at[c], recv_sem=zed_recv.at[c],
                device_id=(me, peer), device_id_type=MESH).start()
            return 0

        lax.fori_loop(1, nz, send, 0)
        if c == 0:
            lax.fori_loop(1, nz, send_count, 0)
        zarr[mz, :, cut(c)] = zout[mz, :, cut(c)]

    def rim_copies(c):
        return [pltpu.make_async_remote_copy(
            src_ref=eout.at[side, :, cut(c)], dst_ref=earr.at[side, :, cut(c)],
            send_sem=rim_send.at[side, c], recv_sem=rim_recv.at[side, c],
            device_id=peer, device_id_type=MESH) for side, peer in ((0, left), (1, right))]

    shape = (mids, LANES)
    lane = lax.broadcasted_iota(jnp.int32, shape, 1)
    sub = lax.broadcasted_iota(jnp.int32, shape, 0)

    def keep(h, at_row, b, part):
        here = pl.ds(b * LANES, LANES)
        xa[h, at_row:at_row + mids, here] = part
        after = xa[h, at_row:at_row + mids, (b + 1) * LANES:(b + 2) * LANES]
        xb[h, at_row:at_row + mids, here] = jnp.where(
            lane < LANES - 1, pltpu.roll(part, LANES - 1, 1), pltpu.roll(after, LANES - 1, 1))

    def sum_chunk(c):
        all_of(zarr.at[pl.ds(0, nz - 1), :, cut(c)], zed_recv.at[c])
        begin, count = plan[c]
        for b in reversed(range(begin, begin + count)):
            here = pl.ds(b * LANES, LANES)
            total = zarr[0, :, here].astype(jnp.float32)
            for z in range(1, nz):
                total = total + zarr[z, :, here].astype(jnp.float32)
            total = total.astype(jnp.bfloat16).astype(jnp.float32)
            for h in range(classes):
                part = total[h * mids:(h + 1) * mids]
                eout[0, h:h + 1, here] = part[0:1]
                eout[1, h:h + 1, here] = part[mids - 1:mids]
                keep(h, 0, b, part)
        for copy in rim_copies(c):
            copy.start()

    is_first = (me == 0) & (mz == 0)
    is_last = (me == inline - 1) & (mz == nz - 1)
    take_right = jnp.where(is_last, 0.0, jnp.where(sub == 0, 1.0, 0.0))
    take_left = jnp.where(is_first, 0.0, jnp.where(sub == mids - 1, 1.0, 0.0))

    def rim_chunk(c):
        for copy in rim_copies(c):
            copy.wait_recv()
        begin, count = plan[c]
        for b in reversed(range(begin, begin + count)):
            here = pl.ds(b * LANES, LANES)
            for h in range(classes):
                keep(h, mids, b, take_right * earr[0, h:h + 1, here] + take_left * earr[1, h:h + 1, here])

    def three(mine, rim):
        up = pltpu.roll(jnp.where(sub == mids - 1, rim, mine), 1, 0)
        down = pltpu.roll(jnp.where(sub == 0, rim, mine), mids - 1, 0)
        return mine + up + down

    def stack_one(g, b, scale):
        total = square_sum = rim_total = rim_square = jnp.zeros(shape, jnp.float32)
        for h in range(classes):
            pair = g * classes + h
            row = pl.ds(pair * blocks + b, 1)
            start = start_s[pair, b]
            near = pl.ds((start >> 7) * LANES, LANES)
            far = pl.ds((start >> 7) * LANES + LANES, LANES)
            mask = lane >= (start & (LANES - 1))
            index = jnp.broadcast_to(at[row, :], shape)
            weight_low = jnp.broadcast_to(low[row, :], shape)
            weight_high = jnp.broadcast_to(high[row, :], shape)
            moved = []
            for top in (0, mids):
                this = jnp.where(mask, xa[h, top:top + mids, near], xa[h, top:top + mids, far])
                after = jnp.where(mask, xb[h, top:top + mids, near], xb[h, top:top + mids, far])
                moved.append(weight_low * take_lanes(this, index) + weight_high * take_lanes(after, index))
            total += moved[0]
            square_sum += moved[0] * moved[0]
            rim_total += moved[1]
            rim_square += moved[1] * moved[1]
        here = pl.ds(pl.multiple_of(g * mids, mids), mids)
        sums[b, here, :] = total * scale
        power[here, (b + 1) * LANES:(b + 2) * LANES] = three(total * total, rim_total * rim_total)
        energy[here, (b + 1) * LANES:(b + 2) * LANES] = three(square_sum, rim_square)

    def stack_chunk(c, scale):
        begin, count = plan[c]
        step = 4 // count

        def some(i, _):
            for k in range(step):
                for b in range(begin, begin + count):
                    stack_one(i * step + k, b, scale)
            return 0

        lax.fori_loop(0, vels // step, some, 0)

    def finish(begin, end):
        width = (end - begin + 2) * LANES

        def window(plane, here):
            value = plane[here, begin * LANES:begin * LANES + width]
            by3 = value + pltpu.roll(value, 1, 1) + pltpu.roll(value, width - 1, 1)
            by9 = by3 + pltpu.roll(by3, 3, 1) + pltpu.roll(by3, width - 3, 1)
            return by9[:, LANES:width - LANES]

        def some(i, _):
            for k in range(4):
                here = pl.ds(pl.multiple_of((i * 4 + k) * mids, mids), mids)
                value = window(power, here) / jnp.maximum(classes * window(energy, here), 1.0)
                for b in range(begin, end):
                    ratio[b, here, :] = value[:, (b - begin) * LANES:(b - begin + 1) * LANES]
            return 0

        lax.fori_loop(0, vels // 4, some, 0)
        for b in range(begin, end):
            here = pl.ds(b * LANES, LANES)
            for m in range(mids):
                for half in range(vels // GROUP):
                    semblance_ref[m, half * GROUP:(half + 1) * GROUP, here] = ratio[
                        b, pl.ds(half * GROUP * mids + m, GROUP, stride=mids), :]
                stacked_ref[m, :, here] = jnp.concatenate([
                    sums[b, pl.ds(half * GROUP * mids + m, GROUP, stride=mids), :]
                    for half in range(vels // GROUP)
                ], axis=0).astype(jnp.bfloat16)

    scale = None
    done = blocks
    for c in range(last + 2):
        if c < last:
            bin_chunk(c)
        if 1 <= c <= last:
            sum_chunk(c - 1)
        if c >= 2:
            if scale is None:
                all_of(carr.at[pl.ds(0, nz - 1)], zed_recv.at[last])
                total = carr[0]
                for z in range(1, nz):
                    total = total + carr[z]
                fold = total[0:mids]
                for h in range(1, classes):
                    fold = fold + total[h * mids:(h + 1) * mids]
                scale = 1.0 / jnp.maximum(fold, 1.0)
            rim_chunk(c - 2)
            stack_chunk(c - 2, scale)
            begin = plan[c - 2][0]
            ready = begin + 1 if begin else 0
            if ready < done:
                finish(ready, done)
                done = ready

    for c in range(last):
        for copy in rim_copies(c):
            copy.wait_send()
        all_of(buf.at[pl.ds(0, (inline - 1) * slots), cut(c)], plane_send.at[c])
        all_of(zout.at[pl.ds(0, nz - 1), :, cut(c)], zed_send.at[c])
    all_of(kout.at[pl.ds(0, inline - 1)], plane_send.at[last])
    all_of(cout.at[pl.ds(0, nz - 1)], zed_send.at[last])


def survey(dims, traces, owners, midpoint, offset_class, offsets, velocities, mids):
    nx, ny, nz = dims
    inline = nx * ny * 2
    rows, samples = traces.shape
    classes, vels = offsets.shape[0], velocities.shape[0]
    capacity = max(2, 2 * rows // (inline * nz))
    slots = nz * capacity
    bins = classes * mids
    blocks = samples // LANES
    last = len(chunks_of(blocks))
    f32, bf16, i32 = jnp.float32, jnp.bfloat16, jnp.int32
    smem = pl.BlockSpec(memory_space=pltpu.SMEM)
    vmem = pl.BlockSpec(memory_space=pltpu.VMEM)
    dma = pltpu.SemaphoreType.DMA
    pairs = vels * classes
    padded = samples + 2 * LANES
    slowness = offsets[None, :] / velocities[:, None]
    time = (jnp.arange(blocks) * LANES).astype(f32)
    position = jnp.sqrt(time * time + (slowness * slowness)[:, :, None])
    start = jnp.minimum(jnp.floor(position), float(samples)).astype(i32).reshape(pairs, blocks)
    return pl.pallas_call(
        functools.partial(kernel, dims),
        out_shape=(
            jax.ShapeDtypeStruct((mids, vels, samples), bf16),
            jax.ShapeDtypeStruct((mids, vels, samples), f32),
        ),
        in_specs=[pl.BlockSpec(memory_space=pl.ANY), vmem, vmem, vmem, smem, smem, smem, vmem],
        out_specs=(vmem, vmem),
        scratch_shapes=[
            pltpu.VMEM((rows, samples), bf16),
            pltpu.VMEM((inline * slots, samples), bf16),
            pltpu.VMEM((inline * slots, samples), bf16),
            pltpu.VMEM((inline, 1, 128), f32),
            pltpu.VMEM((inline, 1, 128), f32),
            pltpu.VMEM((max(inline * slots, nz * bins), max(rows, inline * slots)), bf16),
            pltpu.VMEM((nz, bins, samples), bf16),
            pltpu.VMEM((nz, bins, samples), bf16),
            pltpu.VMEM((nz, bins, 128), f32),
            pltpu.VMEM((nz, bins, 128), f32),
            pltpu.VMEM((2, classes, samples), f32),
            pltpu.VMEM((2, classes, samples), f32),
            pltpu.VMEM((classes, 2 * mids, padded), f32),
            pltpu.VMEM((classes, 2 * mids, padded), f32),
            pltpu.VMEM((pairs * blocks, LANES), i32),
            pltpu.VMEM((pairs * blocks, LANES), f32),
            pltpu.VMEM((pairs * blocks, LANES), f32),
            pltpu.VMEM((vels * mids, padded), f32),
            pltpu.VMEM((vels * mids, padded), f32),
            pltpu.VMEM((blocks, vels * mids, LANES), f32),
            pltpu.VMEM((blocks, vels * mids, LANES), f32),
            dma((last + 1,)), dma((last + 1,)),
            dma((last + 1,)), dma((last + 1,)),
            dma((2, last)), dma((2, last)), dma((2,)),
        ],
        compiler_params=pltpu.CompilerParams(collective_id=0, has_side_effects=True),
        name="survey",
    )(traces, owners, midpoint, offset_class, offsets, velocities, start, start)


def per_device(traces, owners, midpoint, offset_class, offsets, velocities):
    side = round((lax.axis_size("inline") // 2) ** 0.5)
    rows = traces.shape[0]
    return survey(
        (side, side, lax.axis_size("xline")), traces, owners.reshape(1, rows),
        midpoint.reshape(1, rows), offset_class.reshape(1, rows), offsets, velocities, CMP_DEV
    )


def solution(mesh):
    in_specs = (
        P(("inline", "xline"), None),
        P(("inline", "xline"), None),
        P(("inline", "xline")),
        P(("inline", "xline")),
        P(),
        P(),
    )
    out_specs = (P(("inline", "xline"), None, None), P(("inline", "xline"), None, None))
    return jax.shard_map(
        per_device, mesh=mesh, in_specs=in_specs, out_specs=out_specs, check_vma=False
    )
```

```python
import functools

import jax
import jax.numpy as jnp
from jax import lax
from jax.experimental import pallas as pl
from jax.experimental.pallas import tpu as pltpu
from jax.sharding import PartitionSpec as P

CMP_DEV = 8
LANES = 128
GROUP = 8
AHEAD = 3
MESH = pl.DeviceIdType.MESH


def take_lanes(values, index):
    return lax.gather(
        values, index[:, :, None],
        lax.GatherDimensionNumbers(
            offset_dims=(), collapsed_slice_dims=(1,), start_index_map=(1,),
            operand_batching_dims=(0,), start_indices_batching_dims=(0,)),
        slice_sizes=(1, 1), mode=lax.GatherScatterMode.PROMISE_IN_BOUNDS)


def log2(n):
    assert n & (n - 1) == 0
    return n.bit_length() - 1


def chunks_of(blocks):
    sizes = [3] * ((blocks - 4) // 3) + [2, 1, 1]
    assert sum(sizes) == blocks
    out, top = [], blocks
    for size in sizes:
        top -= size
        out.append((top, size))
    return out


def kernel(
    dims, traces_hbm, owner_ref, midpoint_ref, class_ref, offsets_ref, velocities_ref, start_s, start_v,
    stacked_ref, semblance_ref,
    traces, buf, arr, kout, karr, outgoing, member, zout, zarr, cout, carr, eout, earr,
    xs, above, at, low, high, power, energy, sums, ratio,
    plane_send, plane_recv, zed_send, zed_recv, rim_send, rim_recv, own_sem,
):
    nx, ny, nz = dims
    inline = nx * ny * 2
    rows, samples = traces.shape
    slots = buf.shape[0] // inline
    bins = zout.shape[1]
    mids, vels = semblance_ref.shape[:2]
    classes = bins // mids
    blocks = samples // LANES
    plan = chunks_of(blocks)
    last = len(plan)
    me, mz = lax.axis_index("inline"), lax.axis_index("xline")
    mx, my, mc = me >> (log2(ny) + 1), (me >> 1) & (ny - 1), me & 1

    def plane_peer(p):
        q = p >> 1
        tx, ty = q & (nx - 1), q >> log2(nx)
        dx = (nx // 2) ^ tx ^ (tx >> 1)
        dy = (ny // 2) ^ ty ^ (ty >> 1)
        px, py = (mx + dx) & (nx - 1), (my + dy) & (ny - 1)
        return (((px << log2(ny)) | py) << 1) | ((mc + 1 + p) & 1)

    def zed_peer(p):
        step = (p + 1) >> 1
        return (mz + jnp.where((p & 1) == 1, step, nz - step)) & (nz - 1)

    right = ((me + jnp.where(mz == nz - 1, 1, 0)) & (inline - 1), (mz + 1) & (nz - 1))
    left = ((me + jnp.where(mz == 0, inline - 1, 0)) & (inline - 1), (mz + nz - 1) & (nz - 1))

    barrier = pltpu.get_barrier_semaphore()

    def greet_plane(p, _):
        pl.semaphore_signal(barrier, inc=1, device_id=(plane_peer(p), mz), device_id_type=MESH)
        return 0

    def greet_zed(p, _):
        pl.semaphore_signal(barrier, inc=1, device_id=(me, zed_peer(p)), device_id_type=MESH)
        return 0

    traces_in = pltpu.make_async_copy(traces_hbm, traces, own_sem)
    traces_in.start()
    lax.fori_loop(1, nz, greet_zed, 0)
    lax.fori_loop(0, inline - 1, greet_plane, 0)
    for peer in (left, right):
        pl.semaphore_signal(barrier, inc=1, device_id=peer, device_id_type=MESH)

    square = (rows, rows)
    first = lax.broadcasted_iota(jnp.int32, square, 0)
    second = lax.broadcasted_iota(jnp.int32, square, 1)
    owner_row = owner_ref[...]
    owner_all = jnp.broadcast_to(owner_row.astype(jnp.float32), square)
    owner_col = jnp.sum(jnp.where(first == second, owner_all, 0.0), axis=1, keepdims=True)
    same = owner_all == owner_col
    rank_row = jnp.sum(jnp.where(same & (first < second), 1.0, 0.0), axis=0, keepdims=True).astype(jnp.int32)
    rank_col = jnp.sum(jnp.where(same & (second < first), 1.0, 0.0), axis=1, keepdims=True).astype(jnp.int32)
    capacity = slots // nz
    slot_row = owner_row * capacity + rank_row
    wide = (inline * slots, rows)
    outgoing[...] = jnp.where(
        lax.broadcasted_iota(jnp.int32, wide, 0) == slot_row, 1.0, 0.0).astype(jnp.bfloat16)
    per_lane = 128 // slots
    owner_col = owner_col.astype(jnp.int32)
    lane_at = (me & (per_lane - 1)) * slots + (owner_col & (nz - 1)) * capacity + rank_col
    placed = jnp.where(
        lax.broadcasted_iota(jnp.int32, (rows, 128), 1) == lane_at, 1.0, 0.0).astype(jnp.bfloat16)
    key = class_ref[...] * mids + midpoint_ref[...]
    number = ((owner_row & (nz - 1)) * bins + key + 1).astype(jnp.float32)
    chosen = jnp.where(
        lax.broadcasted_iota(jnp.int32, (inline, rows), 0) == owner_row >> log2(nz), number, 0.0
    ).astype(jnp.bfloat16)
    keys = jnp.dot(chosen, placed, preferred_element_type=jnp.float32)
    for i in range(inline):
        kout[i] = keys[i:i + 1, :]

    def cut(c):
        return pl.ds(plan[c][0] * LANES, plan[c][1] * LANES)

    def place(c):
        buf[:, cut(c)] = jnp.dot(
            outgoing[...], traces[:, cut(c)],
            preferred_element_type=jnp.float32).astype(jnp.bfloat16)

    traces_in.wait()
    place(0)
    place(1)

    def prepare(g, _):
        row = lax.broadcasted_iota(jnp.int32, (blocks, LANES), 0)
        lane = lax.broadcasted_iota(jnp.int32, (blocks, LANES), 1)
        time = (row * LANES + lane).astype(jnp.float32)
        diagonal = lax.broadcasted_iota(jnp.int32, (blocks, blocks), 0) == lax.broadcasted_iota(
            jnp.int32, (blocks, blocks), 1)
        speed = jnp.full((1, LANES), velocities_ref[g])
        for h in range(classes):
            slowness = jnp.full((1, LANES), offsets_ref[h]) / speed
            slow = slowness * slowness
            position = jnp.sqrt(time * time + slow)
            starts = jnp.broadcast_to(
                start_v[pl.ds(g * classes + h, 1), :].astype(jnp.float32), (blocks, blocks))
            starts = jnp.sum(jnp.where(diagonal, starts, 0.0), axis=1, keepdims=True)
            floored = jnp.minimum(jnp.floor(position), float(samples))
            floored = jnp.minimum(jnp.maximum(floored, starts), starts + (LANES - 1))
            fraction = position - floored
            index = floored.astype(jnp.int32)
            here = pl.ds(pl.multiple_of((g * classes + h) * blocks, blocks), blocks)
            at[here, :] = index & (LANES - 1)
            low[here, :] = (1.0 - fraction).astype(jnp.bfloat16).astype(jnp.float32)
            high[here, :] = fraction.astype(jnp.bfloat16).astype(jnp.float32)
        return 0

    lax.fori_loop(0, vels, prepare, 0)

    pl.semaphore_wait(barrier, inline - 1 + nz - 1 + 2)

    own = pl.ds(pl.multiple_of(me * slots, slots), slots)

    def send_plane(c):
        def send(p, _):
            peer = plane_peer(p)
            pltpu.make_async_remote_copy(
                src_ref=buf.at[pl.ds(pl.multiple_of(peer * slots, slots), slots), cut(c)],
                dst_ref=arr.at[own, cut(c)],
                send_sem=plane_send.at[c], recv_sem=plane_recv.at[c],
                device_id=(peer, mz), device_id_type=MESH).start()
            return 0
        lax.fori_loop(0, inline - 1, send, 0)

    def send_key(p, _):
        peer = plane_peer(p)
        pltpu.make_async_remote_copy(
            src_ref=kout.at[peer], dst_ref=karr.at[me],
            send_sem=plane_send.at[last], recv_sem=plane_recv.at[last],
            device_id=(peer, mz), device_id_type=MESH).start()
        return 0

    send_plane(0)
    lax.fori_loop(0, inline - 1, send_key, 0)
    send_plane(1)
    for c in range(2, AHEAD):
        place(c)
        send_plane(c)

    for plane in (power, energy):
        plane[:, 0:LANES] = jnp.zeros((vels * mids, LANES), jnp.float32)
        plane[:, LANES + samples:] = jnp.zeros((vels * mids, LANES), jnp.float32)
    for h in range(classes):
        for kind in range(2):
            xs[h, kind, :, samples:] = jnp.zeros((2 * mids, 2 * LANES), jnp.bfloat16)
            above[h, kind] = jnp.zeros((mids, LANES), jnp.float32)

    def all_of(ref, sem):
        pltpu.make_async_copy(ref, ref, sem).wait()

    karr[me] = kout[me]
    all_of(karr.at[pl.ds(0, inline - 1)], plane_recv.at[last])
    arrived = inline * slots
    for q in range(inline // per_lane):
        line = karr[q * per_lane]
        for s in range(1, per_lane):
            line = line + karr[q * per_lane + s]
        number_at = lax.broadcasted_iota(jnp.int32, (nz * bins, 128), 0) + 1
        member[:, q * 128:(q + 1) * 128] = jnp.where(
            line.astype(jnp.int32) == number_at, 1.0, 0.0).astype(jnp.bfloat16)
    counts = jnp.dot(
        member[...], jnp.ones((arrived, 128), jnp.bfloat16),
        preferred_element_type=jnp.float32)
    for z in range(nz):
        cout[z] = counts[z * bins:(z + 1) * bins]
    carr[mz] = cout[mz]

    def send_count(p, _):
        peer = zed_peer(p)
        pltpu.make_async_remote_copy(
            src_ref=cout.at[peer], dst_ref=carr.at[mz],
            send_sem=zed_send.at[last], recv_sem=zed_recv.at[last],
            device_id=(me, peer), device_id_type=MESH).start()
        return 0

    def bin_chunk(c):
        arr[own, cut(c)] = buf[own, cut(c)]
        all_of(arr.at[pl.ds(0, (inline - 1) * slots), cut(c)], plane_recv.at[c])
        part = jnp.dot(
            member[...], arr[:, cut(c)],
            preferred_element_type=jnp.float32).astype(jnp.bfloat16)
        for z in range(nz):
            zout[z, :, cut(c)] = part[z * bins:(z + 1) * bins]

        def send(p, _):
            peer = zed_peer(p)
            pltpu.make_async_remote_copy(
                src_ref=zout.at[peer, :, cut(c)], dst_ref=zarr.at[mz, :, cut(c)],
                send_sem=zed_send.at[c], recv_sem=zed_recv.at[c],
                device_id=(me, peer), device_id_type=MESH).start()
            return 0

        lax.fori_loop(1, nz, send, 0)
        if c == 0:
            lax.fori_loop(1, nz, send_count, 0)
        zarr[mz, :, cut(c)] = zout[mz, :, cut(c)]
        if c + AHEAD < last:
            place(c + AHEAD)
            send_plane(c + AHEAD)

    def rim_copies(c):
        return [pltpu.make_async_remote_copy(
            src_ref=eout.at[side, :, cut(c)], dst_ref=earr.at[side, :, cut(c)],
            send_sem=rim_send.at[side, c], recv_sem=rim_recv.at[side, c],
            device_id=peer, device_id_type=MESH) for side, peer in ((0, left), (1, right))]

    shape = (mids, LANES)
    lane = lax.broadcasted_iota(jnp.int32, shape, 1)
    sub = lax.broadcasted_iota(jnp.int32, shape, 0)
    lane16 = lax.broadcasted_iota(jnp.int32, (2 * mids, LANES), 1).astype(jnp.int16)

    def keep(h, kind, b, part):
        shifted = jnp.where(
            lane < LANES - 1, pltpu.roll(part, LANES - 1, 1), pltpu.roll(above[h, kind], LANES - 1, 1))
        above[h, kind] = part
        xs[h, kind, :, pl.ds(b * LANES, LANES)] = jnp.concatenate(
            [part, shifted], axis=0).astype(jnp.bfloat16)

    def sum_chunk(c):
        all_of(zarr.at[pl.ds(0, nz - 1), :, cut(c)], zed_recv.at[c])
        begin, count = plan[c]
        for b in reversed(range(begin, begin + count)):
            here = pl.ds(b * LANES, LANES)
            total = zarr[0, :, here].astype(jnp.float32)
            for z in range(1, nz):
                total = total + zarr[z, :, here].astype(jnp.float32)
            total = total.astype(jnp.bfloat16).astype(jnp.float32)
            for h in range(classes):
                part = total[h * mids:(h + 1) * mids]
                eout[0, h:h + 1, here] = part[0:1]
                eout[1, h:h + 1, here] = part[mids - 1:mids]
                keep(h, 0, b, part)
        for copy in rim_copies(c):
            copy.start()

    is_first = (me == 0) & (mz == 0)
    is_last = (me == inline - 1) & (mz == nz - 1)
    take_right = jnp.where(is_last, 0.0, jnp.where(sub == 0, 1.0, 0.0))
    take_left = jnp.where(is_first, 0.0, jnp.where(sub == mids - 1, 1.0, 0.0))

    def rim_chunk(c):
        for copy in rim_copies(c):
            copy.wait_recv()
        begin, count = plan[c]
        for b in reversed(range(begin, begin + count)):
            here = pl.ds(b * LANES, LANES)
            for h in range(classes):
                keep(h, 1, b, take_right * earr[0, h:h + 1, here] + take_left * earr[1, h:h + 1, here])

    def three(mine, rim):
        up = pltpu.roll(jnp.where(sub == mids - 1, rim, mine), 1, 0)
        down = pltpu.roll(jnp.where(sub == 0, rim, mine), mids - 1, 0)
        return mine + up + down

    def stack_one(g, b, scale):
        total = square_sum = rim_total = rim_square = jnp.zeros(shape, jnp.float32)
        for h in range(classes):
            pair = g * classes + h
            row = pl.ds(pair * blocks + b, 1)
            start = start_s[pair, b]
            near = pl.ds((start >> 7) * LANES, LANES)
            far = pl.ds((start >> 7) * LANES + LANES, LANES)
            mask = lane16 >= jnp.full((2 * mids, LANES), start & (LANES - 1), jnp.int32).astype(jnp.int16)
            index = jnp.broadcast_to(at[row, :], (2 * mids, LANES)).astype(jnp.int16)
            weight_low = jnp.broadcast_to(low[row, :], shape)
            weight_high = jnp.broadcast_to(high[row, :], shape)
            moved = []
            for kind in range(2):
                picked = take_lanes(
                    jnp.where(mask, xs[h, kind, :, near], xs[h, kind, :, far]), index
                ).astype(jnp.float32)
                moved.append(weight_low * picked[0:mids] + weight_high * picked[mids:])
            total += moved[0]
            square_sum += moved[0] * moved[0]
            rim_total += moved[1]
            rim_square += moved[1] * moved[1]
        here = pl.ds(pl.multiple_of(g * mids, mids), mids)
        sums[b, here, :] = total * scale
        power[here, (b + 1) * LANES:(b + 2) * LANES] = three(total * total, rim_total * rim_total)
        energy[here, (b + 1) * LANES:(b + 2) * LANES] = three(square_sum, rim_square)

    def stack_chunk(c, scale):
        begin, count = plan[c]
        step = {1: 8, 2: 4}.get(count, 2)

        def some(i, _):
            for k in range(step):
                for b in range(begin, begin + count):
                    stack_one(i * step + k, b, scale)
            return 0

        lax.fori_loop(0, vels // step, some, 0)

    def finish(begin, end):
        width = (end - begin + 2) * LANES

        def window(plane, here):
            value = plane[here, begin * LANES:begin * LANES + width]
            by3 = value + pltpu.roll(value, 1, 1) + pltpu.roll(value, width - 1, 1)
            by9 = by3 + pltpu.roll(by3, 3, 1) + pltpu.roll(by3, width - 3, 1)
            return by9[:, LANES:width - LANES]

        def some(i, _):
            for k in range(4):
                here = pl.ds(pl.multiple_of((i * 4 + k) * mids, mids), mids)
                value = window(power, here) / jnp.maximum(classes * window(energy, here), 1.0)
                for b in range(begin, end):
                    ratio[b, here, :] = value[:, (b - begin) * LANES:(b - begin + 1) * LANES]
            return 0

        lax.fori_loop(0, vels // 4, some, 0)
        for b in range(begin, end):
            here = pl.ds(b * LANES, LANES)
            for m in range(mids):
                for half in range(vels // GROUP):
                    semblance_ref[m, half * GROUP:(half + 1) * GROUP, here] = ratio[
                        b, pl.ds(half * GROUP * mids + m, GROUP, stride=mids), :]
                stacked_ref[m, :, here] = jnp.concatenate([
                    sums[b, pl.ds(half * GROUP * mids + m, GROUP, stride=mids), :]
                    for half in range(vels // GROUP)
                ], axis=0).astype(jnp.bfloat16)

    scale = None
    done = blocks
    for c in range(last + 2):
        if c < last:
            bin_chunk(c)
        if 1 <= c <= last:
            sum_chunk(c - 1)
        if c >= 2:
            if scale is None:
                all_of(carr.at[pl.ds(0, nz - 1)], zed_recv.at[last])
                total = carr[0]
                for z in range(1, nz):
                    total = total + carr[z]
                fold = total[0:mids]
                for h in range(1, classes):
                    fold = fold + total[h * mids:(h + 1) * mids]
                scale = 1.0 / jnp.maximum(fold, 1.0)
            rim_chunk(c - 2)
            stack_chunk(c - 2, scale)
            begin = plan[c - 2][0]
            ready = begin + 1 if begin else 0
            if ready < done:
                finish(ready, done)
                done = ready

    for c in range(last):
        for copy in rim_copies(c):
            copy.wait_send()
        all_of(buf.at[pl.ds(0, (inline - 1) * slots), cut(c)], plane_send.at[c])
        all_of(zout.at[pl.ds(0, nz - 1), :, cut(c)], zed_send.at[c])
    all_of(kout.at[pl.ds(0, inline - 1)], plane_send.at[last])
    all_of(cout.at[pl.ds(0, nz - 1)], zed_send.at[last])


def survey(dims, traces, owners, midpoint, offset_class, offsets, velocities, mids):
    nx, ny, nz = dims
    inline = nx * ny * 2
    rows, samples = traces.shape
    classes, vels = offsets.shape[0], velocities.shape[0]
    capacity = max(2, 2 * rows // (inline * nz))
    slots = nz * capacity
    bins = classes * mids
    blocks = samples // LANES
    last = len(chunks_of(blocks))
    f32, bf16, i32 = jnp.float32, jnp.bfloat16, jnp.int32
    smem = pl.BlockSpec(memory_space=pltpu.SMEM)
    vmem = pl.BlockSpec(memory_space=pltpu.VMEM)
    dma = pltpu.SemaphoreType.DMA
    pairs = vels * classes
    padded = samples + 2 * LANES
    slowness = offsets[None, :] / velocities[:, None]
    time = (jnp.arange(blocks) * LANES).astype(f32)
    position = jnp.sqrt(time * time + (slowness * slowness)[:, :, None])
    start = jnp.minimum(jnp.floor(position), float(samples)).astype(i32).reshape(pairs, blocks)
    return pl.pallas_call(
        functools.partial(kernel, dims),
        out_shape=(
            jax.ShapeDtypeStruct((mids, vels, samples), bf16),
            jax.ShapeDtypeStruct((mids, vels, samples), f32),
        ),
        in_specs=[pl.BlockSpec(memory_space=pl.ANY), vmem, vmem, vmem, smem, smem, smem, vmem],
        out_specs=(vmem, vmem),
        scratch_shapes=[
            pltpu.VMEM((rows, samples), bf16),
            pltpu.VMEM((inline * slots, samples), bf16),
            pltpu.VMEM((inline * slots, samples), bf16),
            pltpu.VMEM((inline, 1, 128), f32),
            pltpu.VMEM((inline, 1, 128), f32),
            pltpu.VMEM((inline * slots, rows), bf16),
            pltpu.VMEM((nz * bins, inline * slots), bf16),
            pltpu.VMEM((nz, bins, samples), bf16),
            pltpu.VMEM((nz, bins, samples), bf16),
            pltpu.VMEM((nz, bins, 128), f32),
            pltpu.VMEM((nz, bins, 128), f32),
            pltpu.VMEM((2, classes, samples), f32),
            pltpu.VMEM((2, classes, samples), f32),
            pltpu.VMEM((classes, 2, 2 * mids, padded), bf16),
            pltpu.VMEM((classes, 2, mids, LANES), f32),
            pltpu.VMEM((pairs * blocks, LANES), i32),
            pltpu.VMEM((pairs * blocks, LANES), f32),
            pltpu.VMEM((pairs * blocks, LANES), f32),
            pltpu.VMEM((vels * mids, padded), f32),
            pltpu.VMEM((vels * mids, padded), f32),
            pltpu.VMEM((blocks, vels * mids, LANES), f32),
            pltpu.VMEM((blocks, vels * mids, LANES), f32),
            dma((last + 1,)), dma((last + 1,)),
            dma((last + 1,)), dma((last + 1,)),
            dma((2, last)), dma((2, last)), dma,
        ],
        compiler_params=pltpu.CompilerParams(collective_id=0, has_side_effects=True),
        name="survey",
    )(traces, owners, midpoint, offset_class, offsets, velocities, start, start)


def per_device(traces, owners, midpoint, offset_class, offsets, velocities):
    side = round((lax.axis_size("inline") // 2) ** 0.5)
    rows = traces.shape[0]
    return survey(
        (side, side, lax.axis_size("xline")), traces, owners.reshape(1, rows),
        midpoint.reshape(1, rows), offset_class.reshape(1, rows), offsets, velocities, CMP_DEV
    )


def solution(mesh):
    in_specs = (
        P(("inline", "xline"), None),
        P(("inline", "xline"), None),
        P(("inline", "xline")),
        P(("inline", "xline")),
        P(),
        P(),
    )
    out_specs = (P(("inline", "xline"), None, None), P(("inline", "xline"), None, None))
    return jax.shard_map(
        per_device, mesh=mesh, in_specs=in_specs, out_specs=out_specs, check_vma=False
    )
```

```python
import functools

import jax
import jax.numpy as jnp
from jax import lax
from jax.experimental import pallas as pl
from jax.experimental.pallas import tpu as pltpu
from jax.sharding import PartitionSpec as P

CMP_DEV = 8
LANES = 128
GROUP = 8
HALF_WIN = 4
AHEAD = 8
VMEM_LIMIT = 24 << 20
SUM_LAG = 2
STACK_LAG = 4
SIZES = (1, 2, 3, 3, 3, 2, 1, 1)
MESH = pl.DeviceIdType.MESH


def take_lanes(values, index):
    return lax.gather(
        values, index[:, :, None],
        lax.GatherDimensionNumbers(
            offset_dims=(), collapsed_slice_dims=(1,), start_index_map=(1,),
            operand_batching_dims=(0,), start_indices_batching_dims=(0,)),
        slice_sizes=(1, 1), mode=lax.GatherScatterMode.PROMISE_IN_BOUNDS)


def log2(n):
    assert n & (n - 1) == 0
    return n.bit_length() - 1


def chunks_of(blocks):
    sizes = SIZES if sum(SIZES) == blocks else [1] * blocks
    out, top = [], blocks
    for size in sizes:
        top -= size
        out.append((top, size))
    return out


def kernel(
    dims, traces_hbm, owner_ref, midpoint_ref, class_ref, offsets_ref, velocities_ref, start_s, start_v,
    stacked_ref, semblance_ref,
    traces, buf, arr, kout, karr, outgoing, member, zout, zarr, cout, carr, eout, earr,
    xs, above, at, low, high, planes, band, sums, ratio,
    plane_send, plane_recv, zed_send, zed_recv, rim_send, rim_recv, own_sem,
):
    nx, ny, nz = dims
    inline = nx * ny * 2
    rows, samples = traces.shape
    slots = buf.shape[0] // inline
    bins = zout.shape[1]
    mids, vels = semblance_ref.shape[:2]
    classes = bins // mids
    blocks = samples // LANES
    plan = chunks_of(blocks)
    last = len(plan)
    me, mz = lax.axis_index("inline"), lax.axis_index("xline")
    mx, my, mc = me >> (log2(ny) + 1), (me >> 1) & (ny - 1), me & 1

    def plane_peer(p):
        q = p >> 1
        tx, ty = q & (nx - 1), q >> log2(nx)
        dx = (nx // 2) ^ tx ^ (tx >> 1)
        dy = (ny // 2) ^ ty ^ (ty >> 1)
        px, py = (mx + dx) & (nx - 1), (my + dy) & (ny - 1)
        return (((px << log2(ny)) | py) << 1) | ((mc + 1 + p) & 1)

    def zed_peer(p):
        step = (p + 1) >> 1
        return (mz + jnp.where((p & 1) == 1, step, nz - step)) & (nz - 1)

    right = ((me + jnp.where(mz == nz - 1, 1, 0)) & (inline - 1), (mz + 1) & (nz - 1))
    left = ((me + jnp.where(mz == 0, inline - 1, 0)) & (inline - 1), (mz + nz - 1) & (nz - 1))

    barrier = pltpu.get_barrier_semaphore()

    def greet_plane(p, _):
        pl.semaphore_signal(barrier, inc=1, device_id=(plane_peer(p), mz), device_id_type=MESH)
        return 0

    def greet_zed(p, _):
        pl.semaphore_signal(barrier, inc=1, device_id=(me, zed_peer(p)), device_id_type=MESH)
        return 0

    traces_in = pltpu.make_async_copy(traces_hbm, traces, own_sem)
    traces_in.start()
    lax.fori_loop(1, nz, greet_zed, 0)
    lax.fori_loop(0, inline - 1, greet_plane, 0)
    for peer in (left, right):
        pl.semaphore_signal(barrier, inc=1, device_id=peer, device_id_type=MESH)

    square = (rows, rows)
    first = lax.broadcasted_iota(jnp.int32, square, 0)
    second = lax.broadcasted_iota(jnp.int32, square, 1)
    owner_row = owner_ref[...]
    owner_all = jnp.broadcast_to(owner_row.astype(jnp.float32), square)
    owner_col = jnp.sum(jnp.where(first == second, owner_all, 0.0), axis=1, keepdims=True)
    same = owner_all == owner_col
    rank_row = jnp.sum(jnp.where(same & (first < second), 1.0, 0.0), axis=0, keepdims=True).astype(jnp.int32)
    rank_col = jnp.sum(jnp.where(same & (second < first), 1.0, 0.0), axis=1, keepdims=True).astype(jnp.int32)
    capacity = slots // nz
    slot_row = owner_row * capacity + rank_row
    wide = (inline * slots, rows)
    outgoing[...] = jnp.where(
        lax.broadcasted_iota(jnp.int32, wide, 0) == slot_row, 1.0, 0.0).astype(jnp.bfloat16)
    per_lane = 128 // slots
    owner_col = owner_col.astype(jnp.int32)
    lane_at = (me & (per_lane - 1)) * slots + (owner_col & (nz - 1)) * capacity + rank_col
    placed = jnp.where(
        lax.broadcasted_iota(jnp.int32, (rows, 128), 1) == lane_at, 1.0, 0.0).astype(jnp.bfloat16)
    key = class_ref[...] * mids + midpoint_ref[...]
    number = ((owner_row & (nz - 1)) * bins + key + 1).astype(jnp.float32)
    chosen = jnp.where(
        lax.broadcasted_iota(jnp.int32, (inline, rows), 0) == owner_row >> log2(nz), number, 0.0
    ).astype(jnp.bfloat16)
    keys = jnp.dot(chosen, placed, preferred_element_type=jnp.float32)
    for i in range(inline):
        kout[i] = keys[i:i + 1, :]

    def cut(c):
        return pl.ds(plan[c][0] * LANES, plan[c][1] * LANES)

    def place(c):
        buf[:, cut(c)] = jnp.dot(
            outgoing[...], traces[:, cut(c)],
            preferred_element_type=jnp.float32).astype(jnp.bfloat16)

    traces_in.wait()
    for c in range(last):
        place(c)

    def prepare(g, _):
        row = lax.broadcasted_iota(jnp.int32, (blocks, LANES), 0)
        lane = lax.broadcasted_iota(jnp.int32, (blocks, LANES), 1)
        time = (row * LANES + lane).astype(jnp.float32)
        diagonal = lax.broadcasted_iota(jnp.int32, (blocks, blocks), 0) == lax.broadcasted_iota(
            jnp.int32, (blocks, blocks), 1)
        speed = jnp.full((1, LANES), velocities_ref[g])
        for h in range(classes):
            slowness = jnp.full((1, LANES), offsets_ref[h]) / speed
            slow = slowness * slowness
            position = jnp.sqrt(time * time + slow)
            starts = jnp.broadcast_to(
                start_v[pl.ds(g * classes + h, 1), :].astype(jnp.float32), (blocks, blocks))
            starts = jnp.sum(jnp.where(diagonal, starts, 0.0), axis=1, keepdims=True)
            floored = jnp.minimum(jnp.floor(position), float(samples))
            floored = jnp.minimum(jnp.maximum(floored, starts), starts + (LANES - 1))
            fraction = position - floored
            index = floored.astype(jnp.int32)
            here = pl.ds(pl.multiple_of((g * classes + h) * blocks, blocks), blocks)
            at[here, :] = index & (LANES - 1)
            low[here, :] = (1.0 - fraction).astype(jnp.bfloat16).astype(jnp.float32)
            high[here, :] = fraction.astype(jnp.bfloat16).astype(jnp.float32)
        return 0

    lax.fori_loop(0, vels, prepare, 0)

    for k in range(4):
        planes[k, :, 0:LANES] = jnp.zeros((vels * mids, LANES), jnp.bfloat16)
        planes[k, :, LANES + samples:] = jnp.zeros((vels * mids, LANES), jnp.bfloat16)
    band_shape = (3 * LANES, LANES)
    away = lax.broadcasted_iota(jnp.int32, band_shape, 0) - LANES - lax.broadcasted_iota(
        jnp.int32, band_shape, 1)
    band[...] = jnp.where(
        (away <= HALF_WIN) & (away >= -HALF_WIN), 1.0, 0.0).astype(jnp.bfloat16)
    for h in range(classes):
        for kind in range(2):
            xs[h, kind, :, samples:] = jnp.zeros((2 * mids, 2 * LANES), jnp.bfloat16)
            above[h, kind] = jnp.zeros((mids, LANES), jnp.float32)

    pl.semaphore_wait(barrier, inline - 1 + nz - 1 + 2)

    own = pl.ds(pl.multiple_of(me * slots, slots), slots)

    def several(send):
        def some(i, _):
            for k in range(4):
                send(i * 4 + k, 0)
            return 0
        lax.fori_loop(0, (inline - 1) // 4, some, 0)
        for p in range((inline - 1) // 4 * 4, inline - 1):
            send(p, 0)

    def send_plane(c):
        def send(p, _):
            peer = plane_peer(p)
            pltpu.make_async_remote_copy(
                src_ref=buf.at[pl.ds(pl.multiple_of(peer * slots, slots), slots), cut(c)],
                dst_ref=arr.at[own, cut(c)],
                send_sem=plane_send.at[c], recv_sem=plane_recv.at[c],
                device_id=(peer, mz), device_id_type=MESH).start()
            return 0
        several(send)

    def send_key(p, _):
        peer = plane_peer(p)
        pltpu.make_async_remote_copy(
            src_ref=kout.at[peer], dst_ref=karr.at[me],
            send_sem=plane_send.at[last], recv_sem=plane_recv.at[last],
            device_id=(peer, mz), device_id_type=MESH).start()
        return 0

    several(send_key)
    send_plane(0)
    for c in range(1, min(AHEAD, last)):
        send_plane(c)

    def all_of(ref, sem):
        pltpu.make_async_copy(ref, ref, sem).wait()

    karr[me] = kout[me]
    all_of(karr.at[pl.ds(0, inline - 1)], plane_recv.at[last])
    arrived = inline * slots
    for q in range(inline // per_lane):
        line = karr[q * per_lane]
        for s in range(1, per_lane):
            line = line + karr[q * per_lane + s]
        number_at = lax.broadcasted_iota(jnp.int32, (nz * bins, 128), 0) + 1
        member[:, q * 128:(q + 1) * 128] = jnp.where(
            line.astype(jnp.int32) == number_at, 1.0, 0.0).astype(jnp.bfloat16)
    counts = jnp.dot(
        member[...], jnp.ones((arrived, 128), jnp.bfloat16),
        preferred_element_type=jnp.float32)
    for z in range(nz):
        cout[z] = counts[z * bins:(z + 1) * bins]
    carr[mz] = cout[mz]

    def send_count(p, _):
        peer = zed_peer(p)
        pltpu.make_async_remote_copy(
            src_ref=cout.at[peer], dst_ref=carr.at[mz],
            send_sem=zed_send.at[last], recv_sem=zed_recv.at[last],
            device_id=(me, peer), device_id_type=MESH).start()
        return 0

    def bin_chunk(c):
        arr[own, cut(c)] = buf[own, cut(c)]
        all_of(arr.at[pl.ds(0, (inline - 1) * slots), cut(c)], plane_recv.at[c])
        part = jnp.dot(
            member[...], arr[:, cut(c)],
            preferred_element_type=jnp.float32).astype(jnp.bfloat16)
        for z in range(nz):
            zout[z, :, cut(c)] = part[z * bins:(z + 1) * bins]

        def send(p, _):
            peer = zed_peer(p)
            pltpu.make_async_remote_copy(
                src_ref=zout.at[peer, :, cut(c)], dst_ref=zarr.at[mz, :, cut(c)],
                send_sem=zed_send.at[c], recv_sem=zed_recv.at[c],
                device_id=(me, peer), device_id_type=MESH).start()
            return 0

        lax.fori_loop(1, nz, send, 0)
        if c == 0:
            lax.fori_loop(1, nz, send_count, 0)
        zarr[mz, :, cut(c)] = zout[mz, :, cut(c)]
        if c + AHEAD < last:
            send_plane(c + AHEAD)

    def rim_copies(c):
        return [pltpu.make_async_remote_copy(
            src_ref=eout.at[side, :, cut(c)], dst_ref=earr.at[side, :, cut(c)],
            send_sem=rim_send.at[side, c], recv_sem=rim_recv.at[side, c],
            device_id=peer, device_id_type=MESH) for side, peer in ((0, left), (1, right))]

    shape = (mids, LANES)
    lane = lax.broadcasted_iota(jnp.int32, shape, 1)
    sub = lax.broadcasted_iota(jnp.int32, shape, 0)
    lane16 = lax.broadcasted_iota(jnp.int32, (2 * mids, LANES), 1).astype(jnp.int16)

    def keep(h, kind, b, part):
        shifted = jnp.where(
            lane < LANES - 1, pltpu.roll(part, LANES - 1, 1), pltpu.roll(above[h, kind], LANES - 1, 1))
        above[h, kind] = part
        xs[h, kind, :, pl.ds(b * LANES, LANES)] = jnp.concatenate(
            [part, shifted], axis=0).astype(jnp.bfloat16)

    def sum_chunk(c):
        all_of(zarr.at[pl.ds(0, nz - 1), :, cut(c)], zed_recv.at[c])
        begin, count = plan[c]
        for b in reversed(range(begin, begin + count)):
            here = pl.ds(b * LANES, LANES)
            total = zarr[0, :, here].astype(jnp.float32)
            for z in range(1, nz):
                total = total + zarr[z, :, here].astype(jnp.float32)
            total = total.astype(jnp.bfloat16).astype(jnp.float32)
            for h in range(classes):
                part = total[h * mids:(h + 1) * mids]
                eout[0, h:h + 1, here] = part[0:1]
                eout[1, h:h + 1, here] = part[mids - 1:mids]
                keep(h, 0, b, part)
        for copy in rim_copies(c):
            copy.start()

    is_first = (me == 0) & (mz == 0)
    is_last = (me == inline - 1) & (mz == nz - 1)
    take_right = jnp.where(is_last, 0.0, jnp.where(sub == 0, 1.0, 0.0))
    take_left = jnp.where(is_first, 0.0, jnp.where(sub == mids - 1, 1.0, 0.0))

    def rim_chunk(c):
        for copy in rim_copies(c):
            copy.wait_recv()
        begin, count = plan[c]
        for b in reversed(range(begin, begin + count)):
            here = pl.ds(b * LANES, LANES)
            for h in range(classes):
                keep(h, 1, b, take_right * earr[0, h:h + 1, here] + take_left * earr[1, h:h + 1, here])

    def three(mine, rim):
        up = pltpu.roll(jnp.where(sub == mids - 1, rim, mine), 1, 0)
        down = pltpu.roll(jnp.where(sub == 0, rim, mine), mids - 1, 0)
        return mine + up + down

    def stack_one(g, b, scale):
        total = square_sum = rim_total = rim_square = jnp.zeros(shape, jnp.float32)
        for h in range(classes):
            pair = g * classes + h
            row = pl.ds(pair * blocks + b, 1)
            start = start_s[pair, b]
            near = pl.ds((start >> 7) * LANES, LANES)
            far = pl.ds((start >> 7) * LANES + LANES, LANES)
            mask = lane16 >= jnp.full((2 * mids, LANES), start & (LANES - 1), jnp.int32).astype(jnp.int16)
            index = jnp.broadcast_to(at[row, :], (2 * mids, LANES)).astype(jnp.int16)
            weight_low = jnp.broadcast_to(low[row, :], shape)
            weight_high = jnp.broadcast_to(high[row, :], shape)
            moved = []
            for kind in range(2):
                picked = take_lanes(
                    jnp.where(mask, xs[h, kind, :, near], xs[h, kind, :, far]), index
                ).astype(jnp.float32)
                moved.append(weight_low * picked[0:mids] + weight_high * picked[mids:])
            total += moved[0]
            square_sum += moved[0] * moved[0]
            rim_total += moved[1]
            rim_square += moved[1] * moved[1]
        here = pl.ds(pl.multiple_of(g * mids, mids), mids)
        sums[b, here, :] = total * scale
        return three(total * total, rim_total * rim_total), three(square_sum, rim_square)

    def split(k, pair, b, even, odd):
        here = pl.ds(pl.multiple_of(pair * 2 * mids, 2 * mids), 2 * mids)
        columns = pl.ds((b + 1) * LANES, LANES)
        value = jnp.concatenate([even, odd], axis=0)
        upper = value.astype(jnp.bfloat16)
        planes[2 * k, here, columns] = upper
        planes[2 * k + 1, here, columns] = (value - upper.astype(jnp.float32)).astype(jnp.bfloat16)

    def stack_chunk(c, scale):
        begin, count = plan[c]
        step = {1: 8, 2: 4}.get(count, 2)

        def some(i, _):
            for k in range(step // 2):
                pair = i * (step // 2) + k
                for b in range(begin, begin + count):
                    even = stack_one(pair * 2, b, scale)
                    odd = stack_one(pair * 2 + 1, b, scale)
                    split(0, pair, b, even[0], odd[0])
                    split(1, pair, b, even[1], odd[1])
            return 0

        lax.fori_loop(0, vels // step, some, 0)

    def finish(begin, end):
        def window(k, b):
            columns = pl.ds(b * LANES, 3 * LANES)
            return jnp.dot(
                planes[2 * k, :, columns], band[...], preferred_element_type=jnp.float32
            ) + jnp.dot(
                planes[2 * k + 1, :, columns], band[...], preferred_element_type=jnp.float32)

        for b in range(begin, end):
            ratio[b] = window(0, b) / jnp.maximum(classes * window(1, b), 1.0)
        for b in range(begin, end):
            here = pl.ds(b * LANES, LANES)
            for m in range(mids):
                for half in range(vels // GROUP):
                    semblance_ref[m, half * GROUP:(half + 1) * GROUP, here] = ratio[
                        b, pl.ds(half * GROUP * mids + m, GROUP, stride=mids), :]
                stacked_ref[m, :, here] = jnp.concatenate([
                    sums[b, pl.ds(half * GROUP * mids + m, GROUP, stride=mids), :]
                    for half in range(vels // GROUP)
                ], axis=0).astype(jnp.bfloat16)

    scale = None
    done = blocks
    for c in range(last + STACK_LAG):
        if c < last:
            bin_chunk(c)
        if 0 <= c - SUM_LAG < last:
            sum_chunk(c - SUM_LAG)
        if c >= STACK_LAG:
            if scale is None:
                all_of(carr.at[pl.ds(0, nz - 1)], zed_recv.at[last])
                total = carr[0]
                for z in range(1, nz):
                    total = total + carr[z]
                fold = total[0:mids]
                for h in range(1, classes):
                    fold = fold + total[h * mids:(h + 1) * mids]
                scale = 1.0 / jnp.maximum(fold, 1.0)
            rim_chunk(c - STACK_LAG)
            stack_chunk(c - STACK_LAG, scale)
            begin = plan[c - STACK_LAG][0]
            ready = begin + 1 if begin else 0
            if ready < done:
                finish(ready, done)
                done = ready

    for c in range(last):
        for copy in rim_copies(c):
            copy.wait_send()
        all_of(buf.at[pl.ds(0, (inline - 1) * slots), cut(c)], plane_send.at[c])
        all_of(zout.at[pl.ds(0, nz - 1), :, cut(c)], zed_send.at[c])
    all_of(kout.at[pl.ds(0, inline - 1)], plane_send.at[last])
    all_of(cout.at[pl.ds(0, nz - 1)], zed_send.at[last])


def survey(dims, traces, owners, midpoint, offset_class, offsets, velocities, mids):
    nx, ny, nz = dims
    inline = nx * ny * 2
    rows, samples = traces.shape
    classes, vels = offsets.shape[0], velocities.shape[0]
    capacity = max(2, 2 * rows // (inline * nz))
    slots = nz * capacity
    bins = classes * mids
    blocks = samples // LANES
    last = len(chunks_of(blocks))
    f32, bf16, i32 = jnp.float32, jnp.bfloat16, jnp.int32
    smem = pl.BlockSpec(memory_space=pltpu.SMEM)
    vmem = pl.BlockSpec(memory_space=pltpu.VMEM)
    dma = pltpu.SemaphoreType.DMA
    pairs = vels * classes
    padded = samples + 2 * LANES
    slowness = offsets[None, :] / velocities[:, None]
    time = (jnp.arange(blocks) * LANES).astype(f32)
    position = jnp.sqrt(time * time + (slowness * slowness)[:, :, None])
    start = jnp.minimum(jnp.floor(position), float(samples)).astype(i32).reshape(pairs, blocks)
    return pl.pallas_call(
        functools.partial(kernel, dims),
        out_shape=(
            jax.ShapeDtypeStruct((mids, vels, samples), bf16),
            jax.ShapeDtypeStruct((mids, vels, samples), f32),
        ),
        in_specs=[pl.BlockSpec(memory_space=pl.ANY), vmem, vmem, vmem, smem, smem, smem, vmem],
        out_specs=(vmem, vmem),
        scratch_shapes=[
            pltpu.VMEM((rows, samples), bf16),
            pltpu.VMEM((inline * slots, samples), bf16),
            pltpu.VMEM((inline * slots, samples), bf16),
            pltpu.VMEM((inline, 1, 128), f32),
            pltpu.VMEM((inline, 1, 128), f32),
            pltpu.VMEM((inline * slots, rows), bf16),
            pltpu.VMEM((nz * bins, inline * slots), bf16),
            pltpu.VMEM((nz, bins, samples), bf16),
            pltpu.VMEM((nz, bins, samples), bf16),
            pltpu.VMEM((nz, bins, 128), f32),
            pltpu.VMEM((nz, bins, 128), f32),
            pltpu.VMEM((2, classes, samples), f32),
            pltpu.VMEM((2, classes, samples), f32),
            pltpu.VMEM((classes, 2, 2 * mids, padded), bf16),
            pltpu.VMEM((classes, 2, mids, LANES), f32),
            pltpu.VMEM((pairs * blocks, LANES), i32),
            pltpu.VMEM((pairs * blocks, LANES), f32),
            pltpu.VMEM((pairs * blocks, LANES), f32),
            pltpu.VMEM((4, vels * mids, padded), bf16),
            pltpu.VMEM((3 * LANES, LANES), bf16),
            pltpu.VMEM((blocks, vels * mids, LANES), f32),
            pltpu.VMEM((blocks, vels * mids, LANES), f32),
            dma((last + 1,)), dma((last + 1,)),
            dma((last + 1,)), dma((last + 1,)),
            dma((2, last)), dma((2, last)), dma,
        ],
        compiler_params=pltpu.CompilerParams(collective_id=0, has_side_effects=True, vmem_limit_bytes=VMEM_LIMIT),
        name="survey",
    )(traces, owners, midpoint, offset_class, offsets, velocities, start, start)


def per_device(traces, owners, midpoint, offset_class, offsets, velocities):
    side = round((lax.axis_size("inline") // 2) ** 0.5)
    rows = traces.shape[0]
    return survey(
        (side, side, lax.axis_size("xline")), traces, owners.reshape(1, rows),
        midpoint.reshape(1, rows), offset_class.reshape(1, rows), offsets, velocities, CMP_DEV
    )


def solution(mesh):
    in_specs = (
        P(("inline", "xline"), None),
        P(("inline", "xline"), None),
        P(("inline", "xline")),
        P(("inline", "xline")),
        P(),
        P(),
    )
    out_specs = (P(("inline", "xline"), None, None), P(("inline", "xline"), None, None))
    return jax.shard_map(
        per_device, mesh=mesh, in_specs=in_specs, out_specs=out_specs, check_vma=False
    )
```

```python
import functools

import jax
import jax.numpy as jnp
from jax import lax
from jax.experimental import pallas as pl
from jax.experimental.pallas import tpu as pltpu
from jax.sharding import PartitionSpec as P

CMP_DEV = 8
LANES = 128
GROUP = 8
HALF_WIN = 4
AHEAD = 8
VMEM_LIMIT = 24 << 20
SUM_LAG = 2
STACK_LAG = 4
SIZES = (1, 2, 2, 3, 3, 2, 2, 1)
MESH = pl.DeviceIdType.MESH


def take_lanes(values, index):
    return lax.gather(
        values, index[:, :, None],
        lax.GatherDimensionNumbers(
            offset_dims=(), collapsed_slice_dims=(1,), start_index_map=(1,),
            operand_batching_dims=(0,), start_indices_batching_dims=(0,)),
        slice_sizes=(1, 1), mode=lax.GatherScatterMode.PROMISE_IN_BOUNDS)


def log2(n):
    assert n & (n - 1) == 0
    return n.bit_length() - 1


def chunks_of(blocks):
    sizes = SIZES if sum(SIZES) == blocks else [1] * blocks
    out, top = [], blocks
    for size in sizes:
        top -= size
        out.append((top, size))
    return out


def kernel(
    dims, traces_hbm, owner_ref, midpoint_ref, class_ref, offsets_ref, velocities_ref, start_s, start_v,
    stacked_ref, semblance_ref,
    traces, buf, arr, kout, karr, outgoing, member, zout, zarr, cout, carr, eout, earr,
    xs, above, at, low, high, planes, band, sums, ratio,
    plane_send, plane_recv, zed_send, zed_recv, rim_send, rim_recv, own_sem,
):
    nx, ny, nz = dims
    inline = nx * ny * 2
    rows, samples = traces.shape
    slots = buf.shape[0] // inline
    bins = zout.shape[1]
    mids, vels = semblance_ref.shape[:2]
    classes = bins // mids
    blocks = samples // LANES
    plan = chunks_of(blocks)
    last = len(plan)
    me, mz = lax.axis_index("inline"), lax.axis_index("xline")
    mx, my, mc = me >> (log2(ny) + 1), (me >> 1) & (ny - 1), me & 1

    def plane_peer(p):
        q = p >> 1
        tx, ty = q & (nx - 1), q >> log2(nx)
        dx = (nx // 2) ^ tx ^ (tx >> 1)
        dy = (ny // 2) ^ ty ^ (ty >> 1)
        px, py = (mx + dx) & (nx - 1), (my + dy) & (ny - 1)
        return (((px << log2(ny)) | py) << 1) | ((mc + 1 + p) & 1)

    def zed_peer(p):
        step = (p + 1) >> 1
        return (mz + jnp.where((p & 1) == 1, step, nz - step)) & (nz - 1)

    right = ((me + jnp.where(mz == nz - 1, 1, 0)) & (inline - 1), (mz + 1) & (nz - 1))
    left = ((me + jnp.where(mz == 0, inline - 1, 0)) & (inline - 1), (mz + nz - 1) & (nz - 1))

    barrier = pltpu.get_barrier_semaphore()

    def greet_plane(p, _):
        pl.semaphore_signal(barrier, inc=1, device_id=(plane_peer(p), mz), device_id_type=MESH)
        return 0

    def greet_zed(p, _):
        pl.semaphore_signal(barrier, inc=1, device_id=(me, zed_peer(p)), device_id_type=MESH)
        return 0

    traces_in = pltpu.make_async_copy(traces_hbm, traces, own_sem)
    traces_in.start()
    lax.fori_loop(1, nz, greet_zed, 0)
    lax.fori_loop(0, inline - 1, greet_plane, 0)
    for peer in (left, right):
        pl.semaphore_signal(barrier, inc=1, device_id=peer, device_id_type=MESH)

    square = (rows, rows)
    first = lax.broadcasted_iota(jnp.int32, square, 0)
    second = lax.broadcasted_iota(jnp.int32, square, 1)
    owner_row = owner_ref[...]
    owner_all = jnp.broadcast_to(owner_row.astype(jnp.float32), square)
    owner_col = jnp.sum(jnp.where(first == second, owner_all, 0.0), axis=1, keepdims=True)
    same = owner_all == owner_col
    rank_row = jnp.sum(jnp.where(same & (first < second), 1.0, 0.0), axis=0, keepdims=True).astype(jnp.int32)
    rank_col = jnp.sum(jnp.where(same & (second < first), 1.0, 0.0), axis=1, keepdims=True).astype(jnp.int32)
    capacity = slots // nz
    slot_row = owner_row * capacity + rank_row
    wide = (inline * slots, rows)
    outgoing[...] = jnp.where(
        lax.broadcasted_iota(jnp.int32, wide, 0) == slot_row, 1.0, 0.0).astype(jnp.bfloat16)
    per_lane = 128 // slots
    owner_col = owner_col.astype(jnp.int32)
    lane_at = (me & (per_lane - 1)) * slots + (owner_col & (nz - 1)) * capacity + rank_col
    placed = jnp.where(
        lax.broadcasted_iota(jnp.int32, (rows, 128), 1) == lane_at, 1.0, 0.0).astype(jnp.bfloat16)
    key = class_ref[...] * mids + midpoint_ref[...]
    number = ((owner_row & (nz - 1)) * bins + key + 1).astype(jnp.float32)
    chosen = jnp.where(
        lax.broadcasted_iota(jnp.int32, (inline, rows), 0) == owner_row >> log2(nz), number, 0.0
    ).astype(jnp.bfloat16)
    keys = jnp.dot(chosen, placed, preferred_element_type=jnp.float32)
    for i in range(inline):
        kout[i] = keys[i:i + 1, :]

    def cut(c):
        return pl.ds(plan[c][0] * LANES, plan[c][1] * LANES)

    def place(c):
        buf[:, cut(c)] = jnp.dot(
            outgoing[...], traces[:, cut(c)],
            preferred_element_type=jnp.float32).astype(jnp.bfloat16)

    traces_in.wait()
    for c in range(last):
        place(c)

    def prepare(g, _):
        row = lax.broadcasted_iota(jnp.int32, (blocks, LANES), 0)
        lane = lax.broadcasted_iota(jnp.int32, (blocks, LANES), 1)
        time = (row * LANES + lane).astype(jnp.float32)
        diagonal = lax.broadcasted_iota(jnp.int32, (blocks, blocks), 0) == lax.broadcasted_iota(
            jnp.int32, (blocks, blocks), 1)
        speed = jnp.full((1, LANES), velocities_ref[g])
        for h in range(classes):
            slowness = jnp.full((1, LANES), offsets_ref[h]) / speed
            slow = slowness * slowness
            position = jnp.sqrt(time * time + slow)
            starts = jnp.broadcast_to(
                start_v[pl.ds(g * classes + h, 1), :].astype(jnp.float32), (blocks, blocks))
            starts = jnp.sum(jnp.where(diagonal, starts, 0.0), axis=1, keepdims=True)
            floored = jnp.minimum(jnp.floor(position), float(samples))
            floored = jnp.minimum(jnp.maximum(floored, starts), starts + (LANES - 1))
            fraction = position - floored
            index = floored.astype(jnp.int32)
            here = pl.ds(pl.multiple_of((g * classes + h) * blocks, blocks), blocks)
            at[here, :] = index & (LANES - 1)
            low[here, :] = (1.0 - fraction).astype(jnp.bfloat16).astype(jnp.float32)
            high[here, :] = fraction.astype(jnp.bfloat16).astype(jnp.float32)
        return 0

    lax.fori_loop(0, vels, prepare, 0)

    for k in range(4):
        planes[k, :, 0:LANES] = jnp.zeros((vels * mids, LANES), jnp.bfloat16)
        planes[k, :, LANES + samples:] = jnp.zeros((vels * mids, LANES), jnp.bfloat16)
    band_shape = (3 * LANES, LANES)
    away = lax.broadcasted_iota(jnp.int32, band_shape, 0) - LANES - lax.broadcasted_iota(
        jnp.int32, band_shape, 1)
    band[...] = jnp.where(
        (away <= HALF_WIN) & (away >= -HALF_WIN), 1.0, 0.0).astype(jnp.bfloat16)
    for h in range(classes):
        for kind in range(2):
            xs[h, kind, :, samples:] = jnp.zeros((2 * mids, 2 * LANES), jnp.bfloat16)
            above[h, kind] = jnp.zeros((mids, LANES), jnp.float32)

    pl.semaphore_wait(barrier, inline - 1 + nz - 1 + 2)

    own = pl.ds(pl.multiple_of(me * slots, slots), slots)

    def several(send):
        def some(i, _):
            for k in range(4):
                send(i * 4 + k, 0)
            return 0
        lax.fori_loop(0, (inline - 1) // 4, some, 0)
        for p in range((inline - 1) // 4 * 4, inline - 1):
            send(p, 0)

    def send_plane(c):
        def send(p, _):
            peer = plane_peer(p)
            pltpu.make_async_remote_copy(
                src_ref=buf.at[pl.ds(pl.multiple_of(peer * slots, slots), slots), cut(c)],
                dst_ref=arr.at[own, cut(c)],
                send_sem=plane_send.at[c], recv_sem=plane_recv.at[c],
                device_id=(peer, mz), device_id_type=MESH).start()
            return 0
        several(send)

    def send_key(p, _):
        peer = plane_peer(p)
        pltpu.make_async_remote_copy(
            src_ref=kout.at[peer], dst_ref=karr.at[me],
            send_sem=plane_send.at[last], recv_sem=plane_recv.at[last],
            device_id=(peer, mz), device_id_type=MESH).start()
        return 0

    several(send_key)
    send_plane(0)
    for c in range(1, min(AHEAD, last)):
        send_plane(c)

    def all_of(ref, sem):
        pltpu.make_async_copy(ref, ref, sem).wait()

    karr[me] = kout[me]
    all_of(karr.at[pl.ds(0, inline - 1)], plane_recv.at[last])
    arrived = inline * slots
    for q in range(inline // per_lane):
        line = karr[q * per_lane]
        for s in range(1, per_lane):
            line = line + karr[q * per_lane + s]
        number_at = lax.broadcasted_iota(jnp.int32, (nz * bins, 128), 0) + 1
        member[:, q * 128:(q + 1) * 128] = jnp.where(
            line.astype(jnp.int32) == number_at, 1.0, 0.0).astype(jnp.bfloat16)
    counts = jnp.dot(
        member[...], jnp.ones((arrived, 128), jnp.bfloat16),
        preferred_element_type=jnp.float32)
    for z in range(nz):
        cout[z] = counts[z * bins:(z + 1) * bins]
    carr[mz] = cout[mz]

    def send_count(p, _):
        peer = zed_peer(p)
        pltpu.make_async_remote_copy(
            src_ref=cout.at[peer], dst_ref=carr.at[mz],
            send_sem=zed_send.at[last], recv_sem=zed_recv.at[last],
            device_id=(me, peer), device_id_type=MESH).start()
        return 0

    def bin_chunk(c):
        arr[own, cut(c)] = buf[own, cut(c)]
        all_of(arr.at[pl.ds(0, (inline - 1) * slots), cut(c)], plane_recv.at[c])
        part = jnp.dot(
            member[...], arr[:, cut(c)],
            preferred_element_type=jnp.float32).astype(jnp.bfloat16)
        for z in range(nz):
            zout[z, :, cut(c)] = part[z * bins:(z + 1) * bins]

        def send(p, _):
            peer = zed_peer(p)
            pltpu.make_async_remote_copy(
                src_ref=zout.at[peer, :, cut(c)], dst_ref=zarr.at[mz, :, cut(c)],
                send_sem=zed_send.at[c], recv_sem=zed_recv.at[c],
                device_id=(me, peer), device_id_type=MESH).start()
            return 0

        lax.fori_loop(1, nz, send, 0)
        if c == 0:
            lax.fori_loop(1, nz, send_count, 0)
        zarr[mz, :, cut(c)] = zout[mz, :, cut(c)]
        if c + AHEAD < last:
            send_plane(c + AHEAD)

    def rim_copies(c):
        return [pltpu.make_async_remote_copy(
            src_ref=eout.at[side, :, cut(c)], dst_ref=earr.at[side, :, cut(c)],
            send_sem=rim_send.at[side, c], recv_sem=rim_recv.at[side, c],
            device_id=peer, device_id_type=MESH) for side, peer in ((0, left), (1, right))]

    shape = (mids, LANES)
    lane = lax.broadcasted_iota(jnp.int32, shape, 1)
    sub = lax.broadcasted_iota(jnp.int32, shape, 0)
    lane16 = lax.broadcasted_iota(jnp.int32, (2 * mids, LANES), 1).astype(jnp.int16)

    def keep(h, kind, b, part):
        shifted = jnp.where(
            lane < LANES - 1, pltpu.roll(part, LANES - 1, 1), pltpu.roll(above[h, kind], LANES - 1, 1))
        above[h, kind] = part
        xs[h, kind, :, pl.ds(b * LANES, LANES)] = jnp.concatenate(
            [part, shifted], axis=0).astype(jnp.bfloat16)

    def sum_chunk(c):
        all_of(zarr.at[pl.ds(0, nz - 1), :, cut(c)], zed_recv.at[c])
        begin, count = plan[c]
        for b in reversed(range(begin, begin + count)):
            here = pl.ds(b * LANES, LANES)
            total = zarr[0, :, here].astype(jnp.float32)
            for z in range(1, nz):
                total = total + zarr[z, :, here].astype(jnp.float32)
            total = total.astype(jnp.bfloat16).astype(jnp.float32)
            for h in range(classes):
                part = total[h * mids:(h + 1) * mids]
                eout[0, h:h + 1, here] = part[0:1]
                eout[1, h:h + 1, here] = part[mids - 1:mids]
                keep(h, 0, b, part)
        for copy in rim_copies(c):
            copy.start()

    is_first = (me == 0) & (mz == 0)
    is_last = (me == inline - 1) & (mz == nz - 1)
    take_right = jnp.where(is_last, 0.0, jnp.where(sub == 0, 1.0, 0.0))
    take_left = jnp.where(is_first, 0.0, jnp.where(sub == mids - 1, 1.0, 0.0))

    def rim_chunk(c):
        for copy in rim_copies(c):
            copy.wait_recv()
        begin, count = plan[c]
        for b in reversed(range(begin, begin + count)):
            here = pl.ds(b * LANES, LANES)
            for h in range(classes):
                keep(h, 1, b, take_right * earr[0, h:h + 1, here] + take_left * earr[1, h:h + 1, here])

    def three(mine, rim):
        up = pltpu.roll(jnp.where(sub == mids - 1, rim, mine), 1, 0)
        down = pltpu.roll(jnp.where(sub == 0, rim, mine), mids - 1, 0)
        return mine + up + down

    def stack_one(g, b, scale):
        total = square_sum = rim_total = rim_square = jnp.zeros(shape, jnp.float32)
        for h in range(classes):
            pair = g * classes + h
            row = pl.ds(pair * blocks + b, 1)
            start = start_s[pair, b]
            near = pl.ds((start >> 7) * LANES, LANES)
            far = pl.ds((start >> 7) * LANES + LANES, LANES)
            mask = lane16 >= jnp.full((2 * mids, LANES), start & (LANES - 1), jnp.int32).astype(jnp.int16)
            index = jnp.broadcast_to(at[row, :], (2 * mids, LANES)).astype(jnp.int16)
            weight_low = jnp.broadcast_to(low[row, :], shape)
            weight_high = jnp.broadcast_to(high[row, :], shape)
            moved = []
            for kind in range(2):
                picked = take_lanes(
                    jnp.where(mask, xs[h, kind, :, near], xs[h, kind, :, far]), index
                ).astype(jnp.float32)
                moved.append(weight_low * picked[0:mids] + weight_high * picked[mids:])
            total += moved[0]
            square_sum += moved[0] * moved[0]
            rim_total += moved[1]
            rim_square += moved[1] * moved[1]
        here = pl.ds(pl.multiple_of(g * mids, mids), mids)
        sums[b, here, :] = total * scale
        return three(total * total, rim_total * rim_total), three(square_sum, rim_square)

    def split(k, pair, b, even, odd):
        here = pl.ds(pl.multiple_of(pair * 2 * mids, 2 * mids), 2 * mids)
        columns = pl.ds((b + 1) * LANES, LANES)
        value = jnp.concatenate([even, odd], axis=0)
        upper = value.astype(jnp.bfloat16)
        planes[2 * k, here, columns] = upper
        planes[2 * k + 1, here, columns] = (value - upper.astype(jnp.float32)).astype(jnp.bfloat16)

    def stack_chunk(c, scale):
        begin, count = plan[c]
        step = {1: 8, 2: 4}.get(count, 2)

        def some(i, _):
            for k in range(step // 2):
                pair = i * (step // 2) + k
                for b in range(begin, begin + count):
                    even = stack_one(pair * 2, b, scale)
                    odd = stack_one(pair * 2 + 1, b, scale)
                    split(0, pair, b, even[0], odd[0])
                    split(1, pair, b, even[1], odd[1])
            return 0

        lax.fori_loop(0, vels // step, some, 0)

    def finish(begin, end):
        def window(k, b):
            columns = pl.ds(b * LANES, 3 * LANES)
            return jnp.dot(
                planes[2 * k, :, columns], band[...], preferred_element_type=jnp.float32
            ) + jnp.dot(
                planes[2 * k + 1, :, columns], band[...], preferred_element_type=jnp.float32)

        for b in range(begin, end):
            ratio[b] = window(0, b) / jnp.maximum(classes * window(1, b), 1.0)
        for b in range(begin, end):
            here = pl.ds(b * LANES, LANES)
            for m in range(mids):
                for half in range(vels // GROUP):
                    semblance_ref[m, half * GROUP:(half + 1) * GROUP, here] = ratio[
                        b, pl.ds(half * GROUP * mids + m, GROUP, stride=mids), :]
                stacked_ref[m, :, here] = jnp.concatenate([
                    sums[b, pl.ds(half * GROUP * mids + m, GROUP, stride=mids), :]
                    for half in range(vels // GROUP)
                ], axis=0).astype(jnp.bfloat16)

    scale = None
    done = blocks
    for c in range(last + STACK_LAG):
        if c < last:
            bin_chunk(c)
        if 0 <= c - SUM_LAG < last:
            sum_chunk(c - SUM_LAG)
        if c >= STACK_LAG:
            if scale is None:
                all_of(carr.at[pl.ds(0, nz - 1)], zed_recv.at[last])
                total = carr[0]
                for z in range(1, nz):
                    total = total + carr[z]
                fold = total[0:mids]
                for h in range(1, classes):
                    fold = fold + total[h * mids:(h + 1) * mids]
                scale = 1.0 / jnp.maximum(fold, 1.0)
            rim_chunk(c - STACK_LAG)
            stack_chunk(c - STACK_LAG, scale)
            begin = plan[c - STACK_LAG][0]
            ready = begin + 1 if begin else 0
            if ready < done:
                finish(ready, done)
                done = ready

    for c in range(last):
        for copy in rim_copies(c):
            copy.wait_send()
        all_of(buf.at[pl.ds(0, (inline - 1) * slots), cut(c)], plane_send.at[c])
        all_of(zout.at[pl.ds(0, nz - 1), :, cut(c)], zed_send.at[c])
    all_of(kout.at[pl.ds(0, inline - 1)], plane_send.at[last])
    all_of(cout.at[pl.ds(0, nz - 1)], zed_send.at[last])


def survey(dims, traces, owners, midpoint, offset_class, offsets, velocities, mids):
    nx, ny, nz = dims
    inline = nx * ny * 2
    rows, samples = traces.shape
    classes, vels = offsets.shape[0], velocities.shape[0]
    capacity = max(2, 2 * rows // (inline * nz))
    slots = nz * capacity
    bins = classes * mids
    blocks = samples // LANES
    last = len(chunks_of(blocks))
    f32, bf16, i32 = jnp.float32, jnp.bfloat16, jnp.int32
    smem = pl.BlockSpec(memory_space=pltpu.SMEM)
    vmem = pl.BlockSpec(memory_space=pltpu.VMEM)
    dma = pltpu.SemaphoreType.DMA
    pairs = vels * classes
    padded = samples + 2 * LANES
    slowness = offsets[None, :] / velocities[:, None]
    time = (jnp.arange(blocks) * LANES).astype(f32)
    position = jnp.sqrt(time * time + (slowness * slowness)[:, :, None])
    start = jnp.minimum(jnp.floor(position), float(samples)).astype(i32).reshape(pairs, blocks)
    return pl.pallas_call(
        functools.partial(kernel, dims),
        out_shape=(
            jax.ShapeDtypeStruct((mids, vels, samples), bf16),
            jax.ShapeDtypeStruct((mids, vels, samples), f32),
        ),
        in_specs=[pl.BlockSpec(memory_space=pltpu.HBM), vmem, vmem, vmem, smem, smem, smem, vmem],
        out_specs=(vmem, vmem),
        scratch_shapes=[
            pltpu.VMEM((rows, samples), bf16),
            pltpu.VMEM((inline * slots, samples), bf16),
            pltpu.VMEM((inline * slots, samples), bf16),
            pltpu.VMEM((inline, 1, 128), f32),
            pltpu.VMEM((inline, 1, 128), f32),
            pltpu.VMEM((inline * slots, rows), bf16),
            pltpu.VMEM((nz * bins, inline * slots), bf16),
            pltpu.VMEM((nz, bins, samples), bf16),
            pltpu.VMEM((nz, bins, samples), bf16),
            pltpu.VMEM((nz, bins, 128), f32),
            pltpu.VMEM((nz, bins, 128), f32),
            pltpu.VMEM((2, classes, samples), f32),
            pltpu.VMEM((2, classes, samples), f32),
            pltpu.VMEM((classes, 2, 2 * mids, padded), bf16),
            pltpu.VMEM((classes, 2, mids, LANES), f32),
            pltpu.VMEM((pairs * blocks, LANES), i32),
            pltpu.VMEM((pairs * blocks, LANES), f32),
            pltpu.VMEM((pairs * blocks, LANES), f32),
            pltpu.VMEM((4, vels * mids, padded), bf16),
            pltpu.VMEM((3 * LANES, LANES), bf16),
            pltpu.VMEM((blocks, vels * mids, LANES), f32),
            pltpu.VMEM((blocks, vels * mids, LANES), f32),
            dma((last + 1,)), dma((last + 1,)),
            dma((last + 1,)), dma((last + 1,)),
            dma((2, last)), dma((2, last)), dma,
        ],
        compiler_params=pltpu.CompilerParams(collective_id=0, has_side_effects=True, vmem_limit_bytes=VMEM_LIMIT),
        name="survey",
    )(traces, owners, midpoint, offset_class, offsets, velocities, start, start)


def per_device(traces, owners, midpoint, offset_class, offsets, velocities):
    side = round((lax.axis_size("inline") // 2) ** 0.5)
    rows = traces.shape[0]
    return survey(
        (side, side, lax.axis_size("xline")), traces, owners.reshape(1, rows),
        midpoint.reshape(1, rows), offset_class.reshape(1, rows), offsets, velocities, CMP_DEV
    )


def solution(mesh):
    in_specs = (
        P(("inline", "xline"), None),
        P(("inline", "xline"), None),
        P(("inline", "xline")),
        P(("inline", "xline")),
        P(),
        P(),
    )
    out_specs = (P(("inline", "xline"), None, None), P(("inline", "xline"), None, None))
    return jax.shard_map(
        per_device, mesh=mesh, in_specs=in_specs, out_specs=out_specs, check_vma=False
    )
```

```python
import functools

import jax
import jax.numpy as jnp
from jax import lax
from jax.experimental import pallas as pl
from jax.experimental.pallas import tpu as pltpu
from jax.sharding import PartitionSpec as P

CMP_DEV = 8
LANES = 128
GROUP = 8
HALF_WIN = 4
AHEAD = 5
VMEM_LIMIT = 24 << 20
SUM_LAG = 2
STACK_LAG = 4
SIZES = (1, 2, 2, 3, 3, 2, 2, 1)
MESH = pl.DeviceIdType.MESH


def take_lanes(values, index):
    return lax.gather(
        values, index[:, :, None],
        lax.GatherDimensionNumbers(
            offset_dims=(), collapsed_slice_dims=(1,), start_index_map=(1,),
            operand_batching_dims=(0,), start_indices_batching_dims=(0,)),
        slice_sizes=(1, 1), mode=lax.GatherScatterMode.PROMISE_IN_BOUNDS)


def log2(n):
    assert n & (n - 1) == 0
    return n.bit_length() - 1


def chunks_of(blocks):
    sizes = SIZES if sum(SIZES) == blocks else [1] * blocks
    out, top = [], blocks
    for size in sizes:
        top -= size
        out.append((top, size))
    return out


def kernel(
    dims, traces_hbm, owner_ref, midpoint_ref, class_ref, offsets_ref, velocities_ref, start_s, start_v,
    stacked_ref, semblance_ref,
    traces, buf, arr, kout, karr, outgoing, member, zout, zarr, cout, carr, eout, earr,
    xs, above, at, low, high, planes, band, sums, ratio,
    plane_send, plane_recv, zed_send, zed_recv, rim_send, rim_recv, own_sem,
):
    nx, ny, nz = dims
    inline = nx * ny * 2
    rows, samples = traces.shape
    slots = buf.shape[0] // inline
    bins = zout.shape[1]
    mids, vels = semblance_ref.shape[:2]
    classes = bins // mids
    blocks = samples // LANES
    plan = chunks_of(blocks)
    last = len(plan)
    me, mz = lax.axis_index("inline"), lax.axis_index("xline")
    mx, my, mc = me >> (log2(ny) + 1), (me >> 1) & (ny - 1), me & 1

    def plane_peer(p):
        q = p >> 1
        tx, ty = q & (nx - 1), q >> log2(nx)
        dx = (nx // 2) ^ tx ^ (tx >> 1)
        dy = (ny // 2) ^ ty ^ (ty >> 1)
        px, py = (mx + dx) & (nx - 1), (my + dy) & (ny - 1)
        return (((px << log2(ny)) | py) << 1) | ((mc + 1 + p) & 1)

    def zed_peer(p):
        step = (p + 1) >> 1
        return (mz + jnp.where((p & 1) == 1, step, nz - step)) & (nz - 1)

    right = ((me + jnp.where(mz == nz - 1, 1, 0)) & (inline - 1), (mz + 1) & (nz - 1))
    left = ((me + jnp.where(mz == 0, inline - 1, 0)) & (inline - 1), (mz + nz - 1) & (nz - 1))

    barrier = pltpu.get_barrier_semaphore()

    def greet_plane(p, _):
        pl.semaphore_signal(barrier, inc=1, device_id=(plane_peer(p), mz), device_id_type=MESH)
        return 0

    def greet_zed(p, _):
        pl.semaphore_signal(barrier, inc=1, device_id=(me, zed_peer(p)), device_id_type=MESH)
        return 0

    traces_in = pltpu.make_async_copy(traces_hbm, traces, own_sem)
    traces_in.start()
    lax.fori_loop(1, nz, greet_zed, 0)
    lax.fori_loop(0, inline - 1, greet_plane, 0)
    for peer in (left, right):
        pl.semaphore_signal(barrier, inc=1, device_id=peer, device_id_type=MESH)

    square = (rows, rows)
    first = lax.broadcasted_iota(jnp.int32, square, 0)
    second = lax.broadcasted_iota(jnp.int32, square, 1)
    owner_row = owner_ref[...]
    owner_all = jnp.broadcast_to(owner_row.astype(jnp.float32), square)
    owner_col = jnp.sum(jnp.where(first == second, owner_all, 0.0), axis=1, keepdims=True)
    same = owner_all == owner_col
    rank_row = jnp.sum(jnp.where(same & (first < second), 1.0, 0.0), axis=0, keepdims=True).astype(jnp.int32)
    rank_col = jnp.sum(jnp.where(same & (second < first), 1.0, 0.0), axis=1, keepdims=True).astype(jnp.int32)
    capacity = slots // nz
    slot_row = owner_row * capacity + rank_row
    wide = (inline * slots, rows)
    outgoing[...] = jnp.where(
        lax.broadcasted_iota(jnp.int32, wide, 0) == slot_row, 1.0, 0.0).astype(jnp.bfloat16)
    per_lane = 128 // slots
    owner_col = owner_col.astype(jnp.int32)
    lane_at = (me & (per_lane - 1)) * slots + (owner_col & (nz - 1)) * capacity + rank_col
    placed = jnp.where(
        lax.broadcasted_iota(jnp.int32, (rows, 128), 1) == lane_at, 1.0, 0.0).astype(jnp.bfloat16)
    key = class_ref[...] * mids + midpoint_ref[...]
    number = ((owner_row & (nz - 1)) * bins + key + 1).astype(jnp.float32)
    chosen = jnp.where(
        lax.broadcasted_iota(jnp.int32, (inline, rows), 0) == owner_row >> log2(nz), number, 0.0
    ).astype(jnp.bfloat16)
    keys = jnp.dot(chosen, placed, preferred_element_type=jnp.float32)
    for i in range(inline):
        kout[i] = keys[i:i + 1, :]

    def cut(c):
        return pl.ds(plan[c][0] * LANES, plan[c][1] * LANES)

    def place(c):
        buf[:, cut(c)] = jnp.dot(
            outgoing[...], traces[:, cut(c)],
            preferred_element_type=jnp.float32).astype(jnp.bfloat16)

    traces_in.wait()
    for c in range(last):
        place(c)

    def prepare(g, _):
        row = lax.broadcasted_iota(jnp.int32, (blocks, LANES), 0)
        lane = lax.broadcasted_iota(jnp.int32, (blocks, LANES), 1)
        time = (row * LANES + lane).astype(jnp.float32)
        diagonal = lax.broadcasted_iota(jnp.int32, (blocks, blocks), 0) == lax.broadcasted_iota(
            jnp.int32, (blocks, blocks), 1)
        speed = jnp.full((1, LANES), velocities_ref[g])
        for h in range(classes):
            slowness = jnp.full((1, LANES), offsets_ref[h]) / speed
            slow = slowness * slowness
            position = jnp.sqrt(time * time + slow)
            starts = jnp.broadcast_to(
                start_v[pl.ds(g * classes + h, 1), :].astype(jnp.float32), (blocks, blocks))
            starts = jnp.sum(jnp.where(diagonal, starts, 0.0), axis=1, keepdims=True)
            floored = jnp.minimum(jnp.floor(position), float(samples))
            floored = jnp.minimum(jnp.maximum(floored, starts), starts + (LANES - 1))
            fraction = position - floored
            index = floored.astype(jnp.int32)
            here = pl.ds(pl.multiple_of((g * classes + h) * blocks, blocks), blocks)
            at[here, :] = index & (LANES - 1)
            low[here, :] = (1.0 - fraction).astype(jnp.bfloat16).astype(jnp.float32)
            high[here, :] = fraction.astype(jnp.bfloat16).astype(jnp.float32)
        return 0

    lax.fori_loop(0, vels, prepare, 0)

    for k in range(4):
        planes[k, :, 0:LANES] = jnp.zeros((vels * mids, LANES), jnp.bfloat16)
        planes[k, :, LANES + samples:] = jnp.zeros((vels * mids, LANES), jnp.bfloat16)
    band_shape = (3 * LANES, LANES)
    away = lax.broadcasted_iota(jnp.int32, band_shape, 0) - LANES - lax.broadcasted_iota(
        jnp.int32, band_shape, 1)
    band[...] = jnp.where(
        (away <= HALF_WIN) & (away >= -HALF_WIN), 1.0, 0.0).astype(jnp.bfloat16)
    for h in range(classes):
        for kind in range(2):
            xs[h, kind, :, samples:] = jnp.zeros((2 * mids, 2 * LANES), jnp.bfloat16)
            above[h, kind] = jnp.zeros((mids, LANES), jnp.float32)

    pl.semaphore_wait(barrier, inline - 1 + nz - 1 + 2)

    own = pl.ds(pl.multiple_of(me * slots, slots), slots)

    def several(send):
        def some(i, _):
            for k in range(4):
                send(i * 4 + k, 0)
            return 0
        lax.fori_loop(0, (inline - 1) // 4, some, 0)
        for p in range((inline - 1) // 4 * 4, inline - 1):
            send(p, 0)

    def send_plane(c):
        def send(p, _):
            peer = plane_peer(p)
            pltpu.make_async_remote_copy(
                src_ref=buf.at[pl.ds(pl.multiple_of(peer * slots, slots), slots), cut(c)],
                dst_ref=arr.at[own, cut(c)],
                send_sem=plane_send.at[c], recv_sem=plane_recv.at[c],
                device_id=(peer, mz), device_id_type=MESH).start()
            return 0
        several(send)

    def send_key(p, _):
        peer = plane_peer(p)
        pltpu.make_async_remote_copy(
            src_ref=kout.at[peer], dst_ref=karr.at[me],
            send_sem=plane_send.at[last], recv_sem=plane_recv.at[last],
            device_id=(peer, mz), device_id_type=MESH).start()
        return 0

    several(send_key)
    send_plane(0)
    for c in range(1, min(AHEAD, last)):
        send_plane(c)

    def all_of(ref, sem):
        pltpu.make_async_copy(ref, ref, sem).wait()

    karr[me] = kout[me]
    all_of(karr.at[pl.ds(0, inline - 1)], plane_recv.at[last])
    arrived = inline * slots
    for q in range(inline // per_lane):
        line = karr[q * per_lane]
        for s in range(1, per_lane):
            line = line + karr[q * per_lane + s]
        number_at = lax.broadcasted_iota(jnp.int32, (nz * bins, 128), 0) + 1
        member[:, q * 128:(q + 1) * 128] = jnp.where(
            line.astype(jnp.int32) == number_at, 1.0, 0.0).astype(jnp.bfloat16)
    counts = jnp.dot(
        member[...], jnp.ones((arrived, 128), jnp.bfloat16),
        preferred_element_type=jnp.float32)
    for z in range(nz):
        cout[z] = counts[z * bins:(z + 1) * bins]
    carr[mz] = cout[mz]

    def send_count(p, _):
        peer = zed_peer(p)
        pltpu.make_async_remote_copy(
            src_ref=cout.at[peer], dst_ref=carr.at[mz],
            send_sem=zed_send.at[last], recv_sem=zed_recv.at[last],
            device_id=(me, peer), device_id_type=MESH).start()
        return 0

    def bin_chunk(c):
        arr[own, cut(c)] = buf[own, cut(c)]
        all_of(arr.at[pl.ds(0, (inline - 1) * slots), cut(c)], plane_recv.at[c])
        part = jnp.dot(
            member[...], arr[:, cut(c)],
            preferred_element_type=jnp.float32).astype(jnp.bfloat16)
        for z in range(nz):
            zout[z, :, cut(c)] = part[z * bins:(z + 1) * bins]

        def send(p, _):
            peer = zed_peer(p)
            pltpu.make_async_remote_copy(
                src_ref=zout.at[peer, :, cut(c)], dst_ref=zarr.at[mz, :, cut(c)],
                send_sem=zed_send.at[c], recv_sem=zed_recv.at[c],
                device_id=(me, peer), device_id_type=MESH).start()
            return 0

        lax.fori_loop(1, nz, send, 0)
        if c == 0:
            lax.fori_loop(1, nz, send_count, 0)
        zarr[mz, :, cut(c)] = zout[mz, :, cut(c)]
        if c + AHEAD < last:
            send_plane(c + AHEAD)

    def rim_copies(c):
        return [pltpu.make_async_remote_copy(
            src_ref=eout.at[side, :, cut(c)], dst_ref=earr.at[side, :, cut(c)],
            send_sem=rim_send.at[side, c], recv_sem=rim_recv.at[side, c],
            device_id=peer, device_id_type=MESH) for side, peer in ((0, left), (1, right))]

    shape = (mids, LANES)
    lane = lax.broadcasted_iota(jnp.int32, shape, 1)
    sub = lax.broadcasted_iota(jnp.int32, shape, 0)
    lane16 = lax.broadcasted_iota(jnp.int32, (2 * mids, LANES), 1).astype(jnp.int16)

    def keep(h, kind, b, part):
        shifted = jnp.where(
            lane < LANES - 1, pltpu.roll(part, LANES - 1, 1), pltpu.roll(above[h, kind], LANES - 1, 1))
        above[h, kind] = part
        xs[h, kind, :, pl.ds(b * LANES, LANES)] = jnp.concatenate(
            [part, shifted], axis=0).astype(jnp.bfloat16)

    def sum_chunk(c):
        all_of(zarr.at[pl.ds(0, nz - 1), :, cut(c)], zed_recv.at[c])
        begin, count = plan[c]
        for b in reversed(range(begin, begin + count)):
            here = pl.ds(b * LANES, LANES)
            total = zarr[0, :, here].astype(jnp.float32)
            for z in range(1, nz):
                total = total + zarr[z, :, here].astype(jnp.float32)
            total = total.astype(jnp.bfloat16).astype(jnp.float32)
            for h in range(classes):
                part = total[h * mids:(h + 1) * mids]
                eout[0, h:h + 1, here] = part[0:1]
                eout[1, h:h + 1, here] = part[mids - 1:mids]
                keep(h, 0, b, part)
        for copy in rim_copies(c):
            copy.start()

    is_first = (me == 0) & (mz == 0)
    is_last = (me == inline - 1) & (mz == nz - 1)
    take_right = jnp.where(is_last, 0.0, jnp.where(sub == 0, 1.0, 0.0))
    take_left = jnp.where(is_first, 0.0, jnp.where(sub == mids - 1, 1.0, 0.0))

    def rim_chunk(c):
        for copy in rim_copies(c):
            copy.wait_recv()
        begin, count = plan[c]
        for b in reversed(range(begin, begin + count)):
            here = pl.ds(b * LANES, LANES)
            for h in range(classes):
                keep(h, 1, b, take_right * earr[0, h:h + 1, here] + take_left * earr[1, h:h + 1, here])

    def three(mine, rim):
        up = pltpu.roll(jnp.where(sub == mids - 1, rim, mine), 1, 0)
        down = pltpu.roll(jnp.where(sub == 0, rim, mine), mids - 1, 0)
        return mine + up + down

    def stack_one(g, b, scale):
        total = square_sum = rim_total = rim_square = jnp.zeros(shape, jnp.float32)
        for h in range(classes):
            pair = g * classes + h
            row = pl.ds(pair * blocks + b, 1)
            start = start_s[pair, b]
            near = pl.ds((start >> 7) * LANES, LANES)
            far = pl.ds((start >> 7) * LANES + LANES, LANES)
            mask = lane16 >= jnp.full((2 * mids, LANES), start & (LANES - 1), jnp.int32).astype(jnp.int16)
            index = jnp.broadcast_to(at[row, :], (2 * mids, LANES)).astype(jnp.int16)
            weight_low = jnp.broadcast_to(low[row, :], shape)
            weight_high = jnp.broadcast_to(high[row, :], shape)
            moved = []
            for kind in range(2):
                picked = take_lanes(
                    jnp.where(mask, xs[h, kind, :, near], xs[h, kind, :, far]), index
                ).astype(jnp.float32)
                moved.append(weight_low * picked[0:mids] + weight_high * picked[mids:])
            total += moved[0]
            square_sum += moved[0] * moved[0]
            rim_total += moved[1]
            rim_square += moved[1] * moved[1]
        here = pl.ds(pl.multiple_of(g * mids, mids), mids)
        sums[b, here, :] = total * scale
        return three(total * total, rim_total * rim_total), three(square_sum, rim_square)

    def split(k, pair, b, even, odd):
        here = pl.ds(pl.multiple_of(pair * 2 * mids, 2 * mids), 2 * mids)
        columns = pl.ds((b + 1) * LANES, LANES)
        value = jnp.concatenate([even, odd], axis=0)
        upper = value.astype(jnp.bfloat16)
        planes[2 * k, here, columns] = upper
        planes[2 * k + 1, here, columns] = (value - upper.astype(jnp.float32)).astype(jnp.bfloat16)

    def stack_chunk(c, scale):
        begin, count = plan[c]
        step = {1: 8, 2: 4}.get(count, 2)

        def some(i, _):
            for k in range(step // 2):
                pair = i * (step // 2) + k
                for b in range(begin, begin + count):
                    even = stack_one(pair * 2, b, scale)
                    odd = stack_one(pair * 2 + 1, b, scale)
                    split(0, pair, b, even[0], odd[0])
                    split(1, pair, b, even[1], odd[1])
            return 0

        lax.fori_loop(0, vels // step, some, 0)

    def finish(begin, end):
        def window(k, b):
            columns = pl.ds(b * LANES, 3 * LANES)
            return jnp.dot(
                planes[2 * k, :, columns], band[...], preferred_element_type=jnp.float32
            ) + jnp.dot(
                planes[2 * k + 1, :, columns], band[...], preferred_element_type=jnp.float32)

        for b in range(begin, end):
            ratio[b] = window(0, b) / jnp.maximum(classes * window(1, b), 1.0)
        for b in range(begin, end):
            here = pl.ds(b * LANES, LANES)
            for m in range(mids):
                for half in range(vels // GROUP):
                    semblance_ref[m, half * GROUP:(half + 1) * GROUP, here] = ratio[
                        b, pl.ds(half * GROUP * mids + m, GROUP, stride=mids), :]
                stacked_ref[m, :, here] = jnp.concatenate([
                    sums[b, pl.ds(half * GROUP * mids + m, GROUP, stride=mids), :]
                    for half in range(vels // GROUP)
                ], axis=0).astype(jnp.bfloat16)

    scale = None
    done = blocks
    for c in range(last + STACK_LAG):
        if c < last:
            bin_chunk(c)
        if 0 <= c - SUM_LAG < last:
            sum_chunk(c - SUM_LAG)
        if c >= STACK_LAG:
            if scale is None:
                all_of(carr.at[pl.ds(0, nz - 1)], zed_recv.at[last])
                total = carr[0]
                for z in range(1, nz):
                    total = total + carr[z]
                fold = total[0:mids]
                for h in range(1, classes):
                    fold = fold + total[h * mids:(h + 1) * mids]
                scale = 1.0 / jnp.maximum(fold, 1.0)
            rim_chunk(c - STACK_LAG)
            stack_chunk(c - STACK_LAG, scale)
            begin = plan[c - STACK_LAG][0]
            ready = begin + 1 if begin else 0
            if ready < done:
                finish(ready, done)
                done = ready

    for c in range(last):
        for copy in rim_copies(c):
            copy.wait_send()
        all_of(buf.at[pl.ds(0, (inline - 1) * slots), cut(c)], plane_send.at[c])
        all_of(zout.at[pl.ds(0, nz - 1), :, cut(c)], zed_send.at[c])
    all_of(kout.at[pl.ds(0, inline - 1)], plane_send.at[last])
    all_of(cout.at[pl.ds(0, nz - 1)], zed_send.at[last])


def survey(dims, traces, owners, midpoint, offset_class, offsets, velocities, mids):
    nx, ny, nz = dims
    inline = nx * ny * 2
    rows, samples = traces.shape
    classes, vels = offsets.shape[0], velocities.shape[0]
    capacity = max(2, 2 * rows // (inline * nz))
    slots = nz * capacity
    bins = classes * mids
    blocks = samples // LANES
    last = len(chunks_of(blocks))
    f32, bf16, i32 = jnp.float32, jnp.bfloat16, jnp.int32
    smem = pl.BlockSpec(memory_space=pltpu.SMEM)
    vmem = pl.BlockSpec(memory_space=pltpu.VMEM)
    dma = pltpu.SemaphoreType.DMA
    pairs = vels * classes
    padded = samples + 2 * LANES
    slowness = offsets[None, :] / velocities[:, None]
    time = (jnp.arange(blocks) * LANES).astype(f32)
    position = jnp.sqrt(time * time + (slowness * slowness)[:, :, None])
    start = jnp.minimum(jnp.floor(position), float(samples)).astype(i32).reshape(pairs, blocks)
    return pl.pallas_call(
        functools.partial(kernel, dims),
        out_shape=(
            jax.ShapeDtypeStruct((mids, vels, samples), bf16),
            jax.ShapeDtypeStruct((mids, vels, samples), f32),
        ),
        in_specs=[pl.BlockSpec(memory_space=pltpu.HBM), vmem, vmem, vmem, smem, smem, smem, vmem],
        out_specs=(vmem, vmem),
        scratch_shapes=[
            pltpu.VMEM((rows, samples), bf16),
            pltpu.VMEM((inline * slots, samples), bf16),
            pltpu.VMEM((inline * slots, samples), bf16),
            pltpu.VMEM((inline, 1, 128), f32),
            pltpu.VMEM((inline, 1, 128), f32),
            pltpu.VMEM((inline * slots, rows), bf16),
            pltpu.VMEM((nz * bins, inline * slots), bf16),
            pltpu.VMEM((nz, bins, samples), bf16),
            pltpu.VMEM((nz, bins, samples), bf16),
            pltpu.VMEM((nz, bins, 128), f32),
            pltpu.VMEM((nz, bins, 128), f32),
            pltpu.VMEM((2, classes, samples), f32),
            pltpu.VMEM((2, classes, samples), f32),
            pltpu.VMEM((classes, 2, 2 * mids, padded), bf16),
            pltpu.VMEM((classes, 2, mids, LANES), f32),
            pltpu.VMEM((pairs * blocks, LANES), i32),
            pltpu.VMEM((pairs * blocks, LANES), f32),
            pltpu.VMEM((pairs * blocks, LANES), f32),
            pltpu.VMEM((4, vels * mids, padded), bf16),
            pltpu.VMEM((3 * LANES, LANES), bf16),
            pltpu.VMEM((blocks, vels * mids, LANES), f32),
            pltpu.VMEM((blocks, vels * mids, LANES), f32),
            dma((last + 1,)), dma((last + 1,)),
            dma((last + 1,)), dma((last + 1,)),
            dma((2, last)), dma((2, last)), dma,
        ],
        compiler_params=pltpu.CompilerParams(collective_id=0, has_side_effects=True, vmem_limit_bytes=VMEM_LIMIT),
        name="survey",
    )(pltpu.with_memory_space_constraint(traces, pltpu.HBM), owners, midpoint, offset_class, offsets, velocities, start, start)


def per_device(traces, owners, midpoint, offset_class, offsets, velocities):
    side = round((lax.axis_size("inline") // 2) ** 0.5)
    rows = traces.shape[0]
    return survey(
        (side, side, lax.axis_size("xline")), traces, owners.reshape(1, rows),
        midpoint.reshape(1, rows), offset_class.reshape(1, rows), offsets, velocities, CMP_DEV
    )


def solution(mesh):
    in_specs = (
        P(("inline", "xline"), None),
        P(("inline", "xline"), None),
        P(("inline", "xline")),
        P(("inline", "xline")),
        P(),
        P(),
    )
    out_specs = (P(("inline", "xline"), None, None), P(("inline", "xline"), None, None))
    return jax.shard_map(
        per_device, mesh=mesh, in_specs=in_specs, out_specs=out_specs, check_vma=False
    )
```
